256 devices in a mesh: dom: 64 (over z, x, core), sub: 4 (over y).
Axes of the slice: x: 4, y: 4, z: 8, core: 2. Of those that a mesh axis runs over, the one named last changes fastest.
Arguments:
- source: float32 [32, 1024, 512], P(None, 'dom', 'sub'), may hold values from -100 to 100
- initial: float32 [32, 1024, 512], P(None, 'dom', 'sub'), may hold values from -6 to 6
- lumped_mass: float32 [1024, 512], P('dom', 'sub'), may hold values from 0.25 to 2.5
- node_slots: int32 [6, 1024, 512], P(None, 'dom', 'sub'), may hold values from 0 to 8, as said below
- stiffness: float32 [6, 6, 1024, 512], P(None, None, 'dom', 'sub'), as said below
Outputs:
- new_residual: float32 [32, 1024, 512], P(None, 'dom', 'sub')
- upper_factor: float32 [128, 128], replicated
The draws below stay inside these ranges and needn't reach their ends.
Inputs may be any that keep to these rules, and one draw needn't show every extreme that they name: `node_slots`: the six entries of one element are distinct offsets. `stiffness`: each 6 x 6 element matrix is symmetric and diagonally dominant.
All inputs are finite; a program needn't handle non-finite values.
Results may differ from the reference program's by a relative error of at most 0.012.
Values sent between devices are 32-bit elements; how exact they have to be, the bound alone decides.
No kernel may reach another device: no remote copies, remote signals or barrier semaphores. Data moves between devices by JAX's collectives and lax.ppermute only.
A program may use at most 64 MiB of HBM per device.

```python
import math
import jax
import jax.numpy as jnp
from jax import lax

FIELDS = 32
STEPS = 4
ROWS = 1024
COLS = 512


def draw_source(key, part):
    first_key = jax.random.fold_in(jax.random.fold_in(key, 11), 0)
    rows = jnp.arange(ROWS, dtype=jnp.float32) / float(max(ROWS - 1, 1))
    tent = 1.0 - jnp.abs(2.0 * rows - 1.0)
    values = jax.random.normal(first_key, (FIELDS, ROWS, COLS), jnp.float32)
    values = jnp.clip(values, -6.0, 6.0)
    rise = jnp.exp(math.log(16.0) * tent)
    values = values * rise[None, :, None]
    return values.astype(jnp.float32)


def draw_node_slots(key, part):
    scores = jax.random.randint(key, (9, ROWS, COLS), 0, 65536) * 16 + jnp.arange(9, dtype=jnp.int32)[:, None, None]
    order = jnp.argsort(scores, axis=0)
    return order[:6].astype(jnp.int32)


def draw_stiffness(key, part):
    first_key, second_key = jax.random.split(jax.random.fold_in(key, 7), 2)
    upper_part = jax.random.uniform(first_key, (6, 6, ROWS, COLS), jnp.float32, -0.03, 0.03)
    symmetric = (upper_part + jnp.transpose(upper_part, (1, 0, 2, 3))) * 0.5
    diagonal = 0.15 + 0.1 * jax.random.uniform(second_key, (6, ROWS, COLS), jnp.float32)
    index = jnp.arange(6)
    is_diag = (index[:, None] == index[None, :])[:, :, None, None]
    mats = jnp.where(is_diag, diagonal[:, None], symmetric)
    return mats.astype(jnp.float32)


def steps_of(key, shape, shards, low, high):
    loudness, own = 1.0, jax.random.fold_in(key, 6)
    for dim, shards_of in shards:
        draws = jnp.exp(jax.random.uniform(jax.random.fold_in(own, dim), (shards_of,), jnp.float32, low / len(shards), high / len(shards)))
        loudness = loudness * jnp.repeat(draws, shape[dim] // shards_of).reshape([-1 if axis == dim else 1 for axis in range(len(shape))])
    return loudness


def centred(own_key, shape, width, bound, cuts=(), held_as=jnp.bfloat16):
    loudness = steps_of(own_key, shape, cuts, -0.22, 0.18) if cuts else 1.0
    drawn = jax.random.normal(own_key, shape, jnp.float32) * width * loudness
    return jnp.minimum(jnp.maximum(drawn, -bound), bound).astype(held_as)


def setup_inputs(seed: int = 0) -> dict:
    keys = jax.random.split(jax.random.key(seed), 6)
    return {
        "source": draw_source(jax.random.fold_in(keys[5], 71), 0),
        "initial": centred(keys[1], (FIELDS, ROWS, COLS), 1.0, 6.0, ((1, 64), (2, 4)), jnp.float32),
        "lumped_mass": jnp.clip(jnp.exp(math.log(2.5) - 2.3025851 * jax.random.uniform(keys[2], (ROWS, COLS), jnp.float32) ** steps_of(keys[2], (ROWS, COLS), ((0, 64), (1, 4)), -0.2, 0.2)), 0.25, 2.5),
        "node_slots": draw_node_slots(jax.random.fold_in(keys[5], 71), 0),
        "stiffness": draw_stiffness(jax.random.fold_in(keys[5], 71), 0),
    }


def offset_matrix(node_slots, stiffness):
    result = []
    middle = []
    for target in range(9):
        acc = jnp.zeros(stiffness.shape[1:], jnp.float32)
        for second in range(6):
            acc = acc + stiffness[:, second] * (node_slots[second] == target).astype(jnp.float32)[None]
        middle.append(acc)
    for first_off in range(9):
        for second_off in range(9):
            value = jnp.sum(middle[second_off] * (node_slots == first_off).astype(jnp.float32), axis=0)
            result.append(value)
    return jnp.stack(result, axis=0)

def stencil(padded_k, height, breadth):
    fields = {}
    for first_off in range(9):
        row_p = first_off // 3 - 1
        col_p = first_off % 3 - 1
        for second_off in range(9):
            row_q = second_off // 3 - 1
            col_q = second_off % 3 - 1
            piece = padded_k[first_off * 9 + second_off, 1 - row_p:1 - row_p + height, 1 - col_p:1 - col_p + breadth]
            place = (row_q - row_p, col_q - col_p)
            fields[place] = fields[place] + piece if place in fields else piece
    return sorted(fields.items())

def reference(source, initial, lumped_mass, node_slots, stiffness):
    height, breadth = lumped_mass.shape
    nfield = source.shape[0]
    coeffs = offset_matrix(node_slots, stiffness)
    padded_k = jnp.pad(coeffs, ((0, 0), (1, 1), (1, 1)))
    terms = stencil(padded_k, height, breadth)

    def apply(field):
        wide = jnp.pad(field, ((0, 0), (2, 2), (2, 2)))
        out = lumped_mass[None] * field
        for place, weight in terms:
            out = out + weight[None] * wide[:, 2 + place[0]:2 + place[0] + height, 2 + place[1]:2 + place[1] + breadth]
        return out
    start_residual = source - apply(initial)
    previous = start_residual
    blocks = []
    for step in range(STEPS):
        image = apply(previous)
        blocks.append(image.reshape(nfield, height * breadth))
        previous = image - 2.0 * previous
    basis = jnp.concatenate(blocks, axis=0)
    flat = start_residual.reshape(nfield, height * breadth)
    count = float(height * breadth)
    gram = jnp.dot(basis, basis.T, precision=lax.Precision.HIGHEST) / count
    projected = jnp.dot(basis, flat.T, precision=lax.Precision.HIGHEST) / count
    lower = jnp.linalg.cholesky(gram)
    solved = jax.scipy.linalg.cho_solve((lower, True), projected)
    new_flat = flat - jnp.dot(solved.T, basis, precision=lax.Precision.HIGHEST)
    return (new_flat.reshape(nfield, height, breadth), lower.T)
```

```python
import jax
import jax.numpy as jnp
import numpy as np
from jax import lax
from jax.experimental import pallas as pl
from jax.experimental.pallas import tpu as pltpu
from jax.sharding import Mesh, PartitionSpec as P

STEPS = 4
NF = 32
NR = 16
NC = 128
HALO = 10
INTERPRET = False
F32 = jnp.float32

HALF = [(0, 0), (0, 1), (0, 2)] + [(dr, dc) for dr in (1, 2) for dc in range(-2, 3)]
HALF_INDEX = {d: i for i, d in enumerate(HALF)}
NH = len(HALF)
TURNED = [d for d in HALF if d[1] != 0]
TURNED_INDEX = {d: NH + i for i, d in enumerate(TURNED)}
NCOEF = NH + len(TURNED)


def lanes(shape):
    return lax.broadcasted_iota(jnp.int32, shape, len(shape) - 1)


def turn(value, shift):
    shift = shift % NC
    return value if shift == 0 else pltpu.roll(value, shift, value.ndim - 1)


def call(body, outs, scratch=(), **kw):
    return pl.pallas_call(
        body,
        out_shape=outs,
        scratch_shapes=scratch,
        interpret=INTERPRET,
        **kw,
    )


def vmem_specs(count):
    return [pl.BlockSpec(memory_space=pltpu.VMEM)] * count


def prepare_body(rows_total, cols_total, pos, source, initial, mass, slots, stiffness,
                 ini_x, src_x, w_main, w_strip, to_left, to_right, acc):
    row = lax.broadcasted_iota(jnp.int32, (NR, NC), 0) + pos[0] * NR
    col = lanes((NR, NC)) + pos[1] * NC
    top, bottom = row == 0, row == rows_total - 1
    west, east = col == 0, col == cols_total - 1
    kept = []
    for a in range(6):
        slot = slots[a]
        in_west = (slot == 0) | (slot == 3) | (slot == 6)
        in_east = (slot == 2) | (slot == 5) | (slot == 8)
        outside = (top & (slot < 3)) | (bottom & (slot > 5)) | (west & in_west) | (east & in_east)
        kept.append(jnp.where(outside, 99, slot))
    acc[...] = jnp.zeros(acc.shape, F32)
    zero = jnp.zeros((NR, NC), F32)
    for q in range(9):
        middle = []
        for a in range(6):
            value = zero
            for b in range(6):
                value = jnp.where(kept[b] == q, stiffness[a * 6 + b], value)
            middle.append(value)
        for p in range(q + 1):
            value = zero
            for a in range(6):
                value = jnp.where(kept[a] == p, middle[a], value)
            place = HALF_INDEX[(q // 3 - p // 3, q % 3 - p % 3)]
            start = 7 + p // 3 - 1
            acc[p % 3, place, start:start + NR, :] += value
    acc[1, 0, 7:7 + NR, :] += mass[...]

    lane = lanes((24, NC))
    pack_left = [jnp.zeros((24, NC), F32) for _ in range(2)]
    pack_right = [jnp.zeros((24, NC), F32) for _ in range(2)]
    strips = [jnp.zeros((24, NC), F32) for _ in range(4)]
    for d in range(NH):
        east_turn = turn(acc[2, d], 1)
        west_turn = turn(acc[0, d], -1)
        over_east = jnp.where(lane == 0, east_turn, 0.0)
        over_west = jnp.where(lane == NC - 1, west_turn, 0.0)
        main = acc[1, d] + (east_turn - over_east) + (west_turn - over_west)
        w_main[d] = main
        own = turn(jnp.where(lane < 4, main, 0.0) + over_west, 28)
        own = own + turn(jnp.where(lane >= 124, main, 0.0) + over_east, 4)
        strips[d // 4] = strips[d // 4] + turn(own, 32 * (d % 4))
        k = 16 * (d % 8)
        pack_right[d // 8] = pack_right[d // 8] + turn(jnp.where(lane >= 118, main, 0.0) + over_east, 12 + k)
        pack_left[d // 8] = pack_left[d // 8] + turn(jnp.where(lane < 10, main, 0.0) + over_west, 4 + k)
    for j in range(4):
        w_strip[j] = strips[j]
    for j in range(2):
        to_right[128 + 24 * j:152 + 24 * j, :] = pack_right[j]
        to_left[128 + 24 * j:152 + 24 * j, :] = pack_left[j]

    lane = lanes((8, NC))
    place = lane % 32
    segment = lane // 32
    for r in range(NR):
        right = jnp.zeros((8, NC), F32)
        left = jnp.zeros((8, NC), F32)
        strip_i = jnp.zeros((8, NC), F32)
        strip_s = jnp.zeros((8, NC), F32)
        for g in range(4):
            here = segment == g
            ini = initial[pl.ds(g * 128 + r, 8, stride=NR), :]
            src = source[pl.ds(g * 128 + r, 8, stride=NR), :]
            ini_x[r, 8 * g:8 * g + 8, :] = ini
            src_x[r, 8 * g:8 * g + 8, :] = src
            turned = turn(ini, 4 + 32 * g)
            strip_i = jnp.where(here & (place < 4), turned, strip_i)
            left = jnp.where(here & (place >= 4) & (place < 14), turned, left)
            turned = turn(src, 4 + 32 * g)
            strip_s = jnp.where(here & (place < 4), turned, strip_s)
            left = jnp.where(here & (place >= 20) & (place < 30), turn(src, 20 + 32 * g), left)
            turned = turn(ini, 28 + 32 * g)
            strip_i = jnp.where(here & (place >= 28), turned, strip_i)
            turned = turn(src, 28 + 32 * g)
            strip_s = jnp.where(here & (place >= 28), turned, strip_s)
            right = jnp.where(here & (place >= 18) & (place < 28), turned, right)
            right = jnp.where(here & (place >= 2) & (place < 12), turn(ini, 12 + 32 * g), right)
        ini_x[r, 32:40, :] = strip_i
        src_x[r, 32:40, :] = strip_s
        to_right[8 * r:8 * r + 8, :] = right
        to_left[8 * r:8 * r + 8, :] = left


ROW_I = 0
ROW_S = 10 * 40
ROW_W = ROW_S + 8 * 40
ROW_H = ROW_W + NH * 16
ROW_END = ROW_H + 4 * 16


def columns_body(ini_x, src_x, w_main, w_strip, from_left, from_right,
                 ini_o, src_o, main_o, strip_o, to_up, to_down):
    lane = lanes((8, NC))
    place = lane % 32
    is_left = (place >= 18) & (place < 28)
    is_right = (place >= 4) & (place < 14)
    for r in range(NR):
        left = from_left[8 * r:8 * r + 8, :]
        right = from_right[8 * r:8 * r + 8, :]
        ini_o[r, 0:32, :] = ini_x[r, 0:32, :]
        src_o[r, 0:32, :] = src_x[r, 0:32, :]
        ini_o[r, 32:40, :] = jnp.where(is_left, turn(left, 16), jnp.where(is_right, right, ini_x[r, 32:40, :]))
        src_o[r, 32:40, :] = jnp.where(is_left, left, jnp.where(is_right, turn(right, -16), src_x[r, 32:40, :]))
    lane = lanes((24, NC))
    strips = [w_strip[j] for j in range(4)]
    for d in range(NH):
        k = 16 * (d % 8)
        left = from_left[128 + 24 * (d // 8):152 + 24 * (d // 8), :]
        right = from_right[128 + 24 * (d // 8):152 + 24 * (d // 8), :]
        left = jnp.where((lane >= 18) & (lane <= 28), turn(left, 16 - k), 0.0)
        right = jnp.where((lane >= 3) & (lane <= 13), turn(right, -k), 0.0)
        strips[d // 4] = strips[d // 4] + turn(left + right, 32 * (d % 4))
        main = w_main[d]
        main = main + jnp.where(lane == 0, turn(left, -28), 0.0)
        main = main + jnp.where(lane == NC - 1, turn(right, 124), 0.0)
        main_o[d] = main
        to_up[ROW_W + 16 * d:ROW_W + 16 * d + 16, :] = main[0:16]
        to_down[ROW_W + 16 * d:ROW_W + 16 * d + 16, :] = main[8:24]
    for j in range(4):
        strip_o[j] = strips[j]
        to_up[ROW_H + 16 * j:ROW_H + 16 * j + 16, :] = strips[j][0:16]
        to_down[ROW_H + 16 * j:ROW_H + 16 * j + 16, :] = strips[j][8:24]
    for i in range(10):
        to_up[ROW_I + 40 * i:ROW_I + 40 * i + 40, :] = ini_o[i]
        to_down[ROW_I + 40 * i:ROW_I + 40 * i + 40, :] = ini_o[6 + i]
    for i in range(8):
        to_up[ROW_S + 40 * i:ROW_S + 40 * i + 40, :] = src_o[i]
        to_down[ROW_S + 40 * i:ROW_S + 40 * i + 40, :] = src_o[8 + i]


def basis_body(scale, ini_x, src_x, w_main, w_strip, from_up, from_down, basis, packed,
               coef_m, coef_h, field, sums):
    lane = lanes((8, NC))
    segment = lane // 32
    own = (1, 2, 3)
    for d in range(NH):
        for t in range(5):
            main = None
            strip = None
            parts = []
            if t < 2:
                parts.append((from_up[ROW_W + 16 * d + 8 * t:ROW_W + 16 * d + 8 * t + 8, :],
                              from_up[ROW_H + 16 * (d // 4) + 8 * t:ROW_H + 16 * (d // 4) + 8 * t + 8, :]))
            if t in own:
                parts.append((w_main[d, 8 * t - 8:8 * t, :], w_strip[d // 4, 8 * t - 8:8 * t, :]))
            if t > 2:
                s = 8 * (t - 3)
                parts.append((from_down[ROW_W + 16 * d + s:ROW_W + 16 * d + s + 8, :],
                              from_down[ROW_H + 16 * (d // 4) + s:ROW_H + 16 * (d // 4) + s + 8, :]))
            main = sum(p[0] for p in parts[1:]) + parts[0][0] if len(parts) > 1 else parts[0][0]
            strip = sum(p[1] for p in parts[1:]) + parts[0][1] if len(parts) > 1 else parts[0][1]
            strip = jnp.where(segment == d % 4, strip, 0.0)
            strip = strip + turn(strip, 32)
            strip = strip + turn(strip, 64)
            coef_m[d, 8 * t:8 * t + 8, :] = main
            coef_h[d, 8 * t:8 * t + 8, :] = strip
            dc = HALF[d][1]
            if dc != 0:
                turned = turn(main, dc)
                if dc > 0:
                    turned = jnp.where(lane < dc, turn(strip, dc - 28), turned)
                else:
                    turned = jnp.where(lane >= NC + dc, turn(strip, dc + 124), turned)
                i = TURNED_INDEX[HALF[d]]
                coef_m[i, 8 * t:8 * t + 8, :] = turned
                coef_h[i, 8 * t:8 * t + 8, :] = turn(strip, dc)

    for i in range(10):
        field[0, i] = from_up[ROW_I + 40 * i:ROW_I + 40 * i + 40, :]
        field[0, 26 + i] = from_down[ROW_I + 40 * i:ROW_I + 40 * i + 40, :]
    for i in range(8):
        field[1, 2 + i] = from_up[ROW_S + 40 * i:ROW_S + 40 * i + 40, :]
        field[1, 26 + i] = from_down[ROW_S + 40 * i:ROW_S + 40 * i + 40, :]
    for i in range(NR):
        field[0, 10 + i] = ini_x[i]
        field[1, 10 + i] = src_x[i]

    place = lane % 32

    def image(buffer, r):
        def unit(coef, u):
            near = [field[buffer, r + 10 + dr, 8 * u:8 * u + 8, :] for dr in range(-2, 3)]
            out = None
            for dc in (0, 1, -1, 2, -2):
                part = None
                for dr in range(-2, 3):
                    term = coef[(dr, dc)] * near[dr + 2]
                    part = term if part is None else part + term
                out = part if out is None else out + turn(part, -dc)
            return out

        def spread(ref):
            coef = {}
            for dr in range(-2, 3):
                for dc in range(-2, 3):
                    if (dr, dc) in HALF_INDEX:
                        index = TURNED_INDEX[(dr, dc)] if dc != 0 else HALF_INDEX[(dr, dc)]
                        at = r + 15
                    else:
                        index = HALF_INDEX[(-dr, -dc)]
                        at = r + 15 + dr
                    coef[(dr, dc)] = jnp.broadcast_to(ref[index, pl.ds(at, 1), :], (8, NC))
            return coef

        coef = spread(coef_m)
        mains = [unit(coef, g) for g in range(4)]
        strip = unit(spread(coef_h), 4)
        fixed = strip
        result = []
        for g in range(4):
            here = segment == g
            fixed = jnp.where(here & (place >= 30), turn(mains[g], 32 * g + 28), fixed)
            fixed = jnp.where(here & (place < 2), turn(mains[g], 32 * g + 4), fixed)
            out = jnp.where(lane < 2, turn(strip, 100 - 32 * g), mains[g])
            result.append(jnp.where(lane >= 126, turn(strip, 124 - 32 * g), out))
        return result + [fixed]

    def start_row(i, carry):
        r = i - 8
        units = image(0, r)
        for u in range(5):
            field[2, r + 10, 8 * u:8 * u + 8, :] = field[1, r + 10, 8 * u:8 * u + 8, :] - units[u]
        return carry

    lax.fori_loop(0, 32, start_row, 0)
    for r in range(NR):
        basis[r, 0:32, :] = field[2, r + 10, 0:32, :]
    for step in range(STEPS):
        reach = 6 - 2 * step
        old, new = 2 + step % 2, 3 - step % 2

        def step_row(i, carry, step=step, reach=reach, old=old, new=new):
            r = i - reach
            units = image(old, r)
            if step + 1 < STEPS:
                for u in range(5):
                    field[new, r + 10, 8 * u:8 * u + 8, :] = units[u] - 2.0 * field[old, r + 10, 8 * u:8 * u + 8, :]

            def keep():
                for u in range(4):
                    basis[r, 32 + 32 * step + 8 * u:40 + 32 * step + 8 * u, :] = units[u]

            if reach == 0:
                keep()
            else:
                pl.when((r >= 0) & (r < NR))(keep)
            return carry

        lax.fori_loop(0, NR + 2 * reach, step_row, 0)

    sums[...] = jnp.zeros(sums.shape, F32)

    def product(i, carry):
        pair = jnp.concatenate([basis[2 * i], basis[2 * i + 1]], axis=1)
        sums[...] += lax.dot_general(pair, pair[32:], (((1,), (1,)), ((), ())),
                                     precision=lax.Precision.HIGHEST, preferred_element_type=F32)
        return carry

    lax.fori_loop(0, NR // 2, product, 0)
    lane = lanes((32, NC))
    odd = jnp.zeros((32, NC), F32)
    even = jnp.zeros((32, NC), F32)
    for b in range(4):
        odd = jnp.where(lane // 32 == b, sums[32 * b:32 * b + 32, :], odd)
        even = jnp.where(lane // 32 == b, sums[32 + 32 * b:64 + 32 * b, :], even)
    odd = odd * scale
    even = even * scale
    row = lax.broadcasted_iota(jnp.int32, (32, NC), 0)
    within = lane % 32
    packed[0:32, :] = jnp.where(within >= row, odd, even)
    diagonal = jnp.sum(jnp.where(within == row, even, 0.0), axis=0, keepdims=True)
    packed[32:40, :] = jnp.broadcast_to(diagonal, (8, NC))


def solve_body(parts, basis, out, upper):
    total = parts[0]
    for i in range(1, parts.shape[0]):
        total = total + parts[i]
    half = total[0:32]
    lane = lanes((32, NC))
    row = lax.broadcasted_iota(jnp.int32, (32, NC), 0)
    within = lane % 32
    block = lane // 32
    flipped = jnp.transpose(jnp.concatenate([half] * 4, axis=0))
    mirror = flipped[0:32]
    for b in range(1, 4):
        mirror = jnp.where(block == b, flipped[32 * b:32 * b + 32], mirror)
    odd = jnp.where(within >= row, half, mirror)
    even = jnp.where(within < row, half, jnp.where(within > row, mirror, jnp.broadcast_to(total[32:33], (32, NC))))

    def pick(a, b, c, d):
        return jnp.where(block == 0, a, jnp.where(block == 1, b, jnp.where(block == 2, c, d)))

    odd_up, odd_down, even_up, even_down = turn(odd, 32), turn(odd, -32), turn(even, 32), turn(even, -32)
    gram = [
        pick(even, odd, even_up, odd_up),
        pick(odd_down, even, odd, even_up),
        pick(even_down, odd_down, even, odd),
        pick(turn(odd, -64), even_down, odd_down, even),
    ]
    first = jnp.where(lane < 32, odd, 0.0)
    second = jnp.where(lane < 32, even, 0.0) - 2.0 * first
    third = jnp.where(lane < 32, odd_down, 0.0) - 2.0 * second
    fourth = jnp.where(lane < 32, even_down, 0.0) - 2.0 * third
    right = [first, second, third, fourth]
    g = [gram[t // 4][8 * (t % 4):8 * (t % 4) + 8] for t in range(16)]
    p = [right[t // 4][8 * (t % 4):8 * (t % 4) + 8] for t in range(16)]
    lane = lanes((8, NC))
    sub = lax.broadcasted_iota(jnp.int32, (8, NC), 0)
    for k in range(128):
        t, j = divmod(k, 8)
        u = jnp.broadcast_to(g[t][j:j + 1, :], (8, NC))
        up = jnp.broadcast_to(p[t][j:j + 1, :], (8, NC))
        d = jnp.broadcast_to(u[:, k:k + 1], (8, NC))
        inverse = 1.0 / d
        line = jnp.where(lane >= k, u / jnp.sqrt(d), 0.0)
        upper[k:k + 1, :] = line[0:1]
        for i in range(16):
            m = jnp.broadcast_to(g[i][:, k:k + 1], (8, NC)) * inverse
            if i == t:
                g[i] = jnp.where(sub == j, g[i] * inverse, g[i] - m * u)
                p[i] = jnp.where(sub == j, p[i] * inverse, p[i] - m * up)
            else:
                g[i] = g[i] - m * u
                p[i] = p[i] - m * up
    weights = jnp.transpose(jnp.concatenate(p, axis=0))[0:32]
    for r in range(NR):
        moved = jnp.dot(weights, basis[r, 32:160, :], precision=lax.Precision.HIGHEST, preferred_element_type=F32)
        out[pl.ds(r, 32, stride=NR), :] = basis[r, 0:32, :] - moved


def shape(*dims):
    return jax.ShapeDtypeStruct(dims, F32)


def neighbours(count, step):
    return [(i, i + step) for i in range(count) if 0 <= i + step < count]


def on_device(dom, sub, dom_count, sub_count, reduce_groups, source, initial, lumped_mass, node_slots, stiffness):
    rows_total, cols_total = dom_count * NR, sub_count * NC
    pos = jnp.stack([lax.axis_index(dom), lax.axis_index(sub)]).astype(jnp.int32)

    def prepare(*refs):
        prepare_body(rows_total, cols_total, *refs)

    ini_x, src_x, w_main, w_strip, to_left, to_right = call(
        prepare,
        (shape(NR, 40, NC), shape(NR, 40, NC), shape(NH, 24, NC), shape(4, 24, NC), shape(176, NC), shape(176, NC)),
        scratch=[pltpu.VMEM((3, NH, 24, NC), F32)],
        in_specs=[pl.BlockSpec(memory_space=pltpu.SMEM)] + vmem_specs(5),
        out_specs=tuple(vmem_specs(6)),
        name="prepare",
    )(pos, source.reshape(NF * NR, NC), initial.reshape(NF * NR, NC), lumped_mass, node_slots,
      stiffness.reshape(36, NR, NC))
    from_right = lax.ppermute(to_left, sub, neighbours(sub_count, -1))
    from_left = lax.ppermute(to_right, sub, neighbours(sub_count, 1))
    ini_x, src_x, w_main, w_strip, to_up, to_down = call(
        columns_body,
        (shape(NR, 40, NC), shape(NR, 40, NC), shape(NH, 24, NC), shape(4, 24, NC), shape(ROW_END, NC),
         shape(ROW_END, NC)),
        name="columns",
    )(ini_x, src_x, w_main, w_strip, from_left, from_right)
    from_down = lax.ppermute(to_up, dom, neighbours(dom_count, -1))
    from_up = lax.ppermute(to_down, dom, neighbours(dom_count, 1))

    def products(*refs):
        basis_body(1.0 / float(rows_total * cols_total), *refs)

    basis, packed = call(
        products,
        (shape(NR, 160, NC), shape(40, NC)),
        scratch=[
            pltpu.VMEM((NCOEF, 40, NC), F32),
            pltpu.VMEM((NCOEF, 40, NC), F32),
            pltpu.VMEM((4, 36, 40, NC), F32),
            pltpu.VMEM((160, NC), F32),
        ],
        name="products",
    )(ini_x, src_x, w_main, w_strip, from_up, from_down)
    for i, (axes, count) in enumerate(reduce_groups):
        if count == 2:
            gathered = jnp.stack([packed, lax.ppermute(packed, axes, [(0, 1), (1, 0)])])
        else:
            gathered = lax.all_to_all(jnp.broadcast_to(packed[None], (count, 40, NC)), axes, 0, 0)
        if i + 1 < len(reduce_groups):
            packed = jnp.sum(gathered, axis=0)
    new_residual, upper = call(
        solve_body,
        (shape(NF * NR, NC), shape(128, 128)),
        name="solve",
    )(gathered, basis)
    return (new_residual.reshape(NF, NR, NC), upper)


def solution(mesh):
    dom_count, sub_count = mesh.shape["dom"], mesh.shape["sub"]
    if dom_count == 64 and sub_count == 4:
        fine = Mesh(mesh.devices.reshape(8, 4, 2, 4), ("z", "x", "c", "sub"))
        dom = ("z", "x", "c")
        groups = ((("c",), 2), (("x", "sub"), 16), (("z",), 8))
    else:
        fine, dom = mesh, ("dom",)
        groups = (("sub", sub_count), ("dom", dom_count))

    def body(*args):
        return on_device(dom, "sub", dom_count, sub_count, groups, *args)

    return jax.shard_map(
        body,
        mesh=fine,
        in_specs=(
            P(None, dom, "sub"),
            P(None, dom, "sub"),
            P(dom, "sub"),
            P(None, dom, "sub"),
            P(None, None, dom, "sub"),
        ),
        out_specs=(P(None, dom, "sub"), P()),
        check_vma=False,
    )
```

```python
import jax
import jax.numpy as jnp
import numpy as np
from jax import lax
from jax.experimental import pallas as pl
from jax.experimental.pallas import tpu as pltpu
from jax.sharding import Mesh, PartitionSpec as P

STEPS = 4
NF = 32
NR = 16
NC = 128
HALO = 10
INTERPRET = False
F32 = jnp.float32

HALF = [(0, 0), (0, 1), (0, 2)] + [(dr, dc) for dr in (1, 2) for dc in range(-2, 3)]
HALF_INDEX = {d: i for i, d in enumerate(HALF)}
NH = len(HALF)
TURNED = [d for d in HALF if d[1] != 0]
TURNED_INDEX = {d: NH + i for i, d in enumerate(TURNED)}
NCOEF = NH + len(TURNED)


def lanes(shape):
    return lax.broadcasted_iota(jnp.int32, shape, len(shape) - 1)


def turn(value, shift):
    shift = shift % NC
    return value if shift == 0 else pltpu.roll(value, shift, value.ndim - 1)


def call(body, outs, scratch=(), **kw):
    return pl.pallas_call(
        body,
        out_shape=outs,
        scratch_shapes=scratch,
        interpret=INTERPRET,
        **kw,
    )


def vmem_specs(count):
    return [pl.BlockSpec(memory_space=pltpu.VMEM)] * count


def prepare_body(rows_total, cols_total, pos, source, initial, mass, slots, stiffness,
                 ini_x, src_x, w_main, w_strip, to_left, to_right, acc):
    row = lax.broadcasted_iota(jnp.int32, (NR, NC), 0) + pos[0] * NR
    col = lanes((NR, NC)) + pos[1] * NC
    top, bottom = row == 0, row == rows_total - 1
    west, east = col == 0, col == cols_total - 1
    kept = []
    for a in range(6):
        slot = slots[a]
        in_west = (slot == 0) | (slot == 3) | (slot == 6)
        in_east = (slot == 2) | (slot == 5) | (slot == 8)
        outside = (top & (slot < 3)) | (bottom & (slot > 5)) | (west & in_west) | (east & in_east)
        kept.append(jnp.where(outside, 99, slot))
    acc[...] = jnp.zeros(acc.shape, F32)
    zero = jnp.zeros((NR, NC), F32)
    for q in range(9):
        middle = []
        for a in range(6):
            value = zero
            for b in range(6):
                value = jnp.where(kept[b] == q, stiffness[a * 6 + b], value)
            middle.append(value)
        for p in range(q + 1):
            value = zero
            for a in range(6):
                value = jnp.where(kept[a] == p, middle[a], value)
            place = HALF_INDEX[(q // 3 - p // 3, q % 3 - p % 3)]
            start = 7 + p // 3 - 1
            acc[p % 3, place, start:start + NR, :] += value
    acc[1, 0, 7:7 + NR, :] += mass[...]

    lane = lanes((24, NC))
    pack_left = [jnp.zeros((24, NC), F32) for _ in range(2)]
    pack_right = [jnp.zeros((24, NC), F32) for _ in range(2)]
    strips = [jnp.zeros((24, NC), F32) for _ in range(4)]
    for d in range(NH):
        east_turn = turn(acc[2, d], 1)
        west_turn = turn(acc[0, d], -1)
        over_east = jnp.where(lane == 0, east_turn, 0.0)
        over_west = jnp.where(lane == NC - 1, west_turn, 0.0)
        main = acc[1, d] + (east_turn - over_east) + (west_turn - over_west)
        w_main[d] = main
        own = turn(jnp.where(lane < 4, main, 0.0) + over_west, 28)
        own = own + turn(jnp.where(lane >= 124, main, 0.0) + over_east, 4)
        strips[d // 4] = strips[d // 4] + turn(own, 32 * (d % 4))
        k = 16 * (d % 8)
        pack_right[d // 8] = pack_right[d // 8] + turn(jnp.where(lane >= 118, main, 0.0) + over_east, 12 + k)
        pack_left[d // 8] = pack_left[d // 8] + turn(jnp.where(lane < 10, main, 0.0) + over_west, 4 + k)
    for j in range(4):
        w_strip[j] = strips[j]
    for j in range(2):
        to_right[128 + 24 * j:152 + 24 * j, :] = pack_right[j]
        to_left[128 + 24 * j:152 + 24 * j, :] = pack_left[j]

    lane = lanes((8, NC))
    place = lane % 32
    segment = lane // 32
    for r in range(NR):
        right = jnp.zeros((8, NC), F32)
        left = jnp.zeros((8, NC), F32)
        strip_i = jnp.zeros((8, NC), F32)
        strip_s = jnp.zeros((8, NC), F32)
        for g in range(4):
            here = segment == g
            ini = initial[pl.ds(g * 128 + r, 8, stride=NR), :]
            src = source[pl.ds(g * 128 + r, 8, stride=NR), :]
            ini_x[r, 8 * g:8 * g + 8, :] = ini
            src_x[r, 8 * g:8 * g + 8, :] = src
            turned = turn(ini, 4 + 32 * g)
            strip_i = jnp.where(here & (place < 4), turned, strip_i)
            left = jnp.where(here & (place >= 4) & (place < 14), turned, left)
            turned = turn(src, 4 + 32 * g)
            strip_s = jnp.where(here & (place < 4), turned, strip_s)
            left = jnp.where(here & (place >= 20) & (place < 30), turn(src, 20 + 32 * g), left)
            turned = turn(ini, 28 + 32 * g)
            strip_i = jnp.where(here & (place >= 28), turned, strip_i)
            turned = turn(src, 28 + 32 * g)
            strip_s = jnp.where(here & (place >= 28), turned, strip_s)
            right = jnp.where(here & (place >= 18) & (place < 28), turned, right)
            right = jnp.where(here & (place >= 2) & (place < 12), turn(ini, 12 + 32 * g), right)
        ini_x[r, 32:40, :] = strip_i
        src_x[r, 32:40, :] = strip_s
        to_right[8 * r:8 * r + 8, :] = right
        to_left[8 * r:8 * r + 8, :] = left


ROW_I = 0
ROW_S = 10 * 40
ROW_W = ROW_S + 8 * 40
ROW_H = ROW_W + NH * 16
ROW_END = ROW_H + 4 * 16


def columns_body(ini_x, src_x, w_main, w_strip, from_left, from_right,
                 ini_o, src_o, main_o, strip_o, to_up, to_down):
    lane = lanes((8, NC))
    place = lane % 32
    is_left = (place >= 18) & (place < 28)
    is_right = (place >= 4) & (place < 14)
    for r in range(NR):
        left = from_left[8 * r:8 * r + 8, :]
        right = from_right[8 * r:8 * r + 8, :]
        ini_o[r, 0:32, :] = ini_x[r, 0:32, :]
        src_o[r, 0:32, :] = src_x[r, 0:32, :]
        ini_o[r, 32:40, :] = jnp.where(is_left, turn(left, 16), jnp.where(is_right, right, ini_x[r, 32:40, :]))
        src_o[r, 32:40, :] = jnp.where(is_left, left, jnp.where(is_right, turn(right, -16), src_x[r, 32:40, :]))
    lane = lanes((24, NC))
    strips = [w_strip[j] for j in range(4)]
    for d in range(NH):
        k = 16 * (d % 8)
        left = from_left[128 + 24 * (d // 8):152 + 24 * (d // 8), :]
        right = from_right[128 + 24 * (d // 8):152 + 24 * (d // 8), :]
        left = jnp.where((lane >= 18) & (lane <= 28), turn(left, 16 - k), 0.0)
        right = jnp.where((lane >= 3) & (lane <= 13), turn(right, -k), 0.0)
        strips[d // 4] = strips[d // 4] + turn(left + right, 32 * (d % 4))
        main = w_main[d]
        main = main + jnp.where(lane == 0, turn(left, -28), 0.0)
        main = main + jnp.where(lane == NC - 1, turn(right, 124), 0.0)
        main_o[d] = main
        to_up[ROW_W + 16 * d:ROW_W + 16 * d + 16, :] = main[0:16]
        to_down[ROW_W + 16 * d:ROW_W + 16 * d + 16, :] = main[8:24]
    for j in range(4):
        strip_o[j] = strips[j]
        to_up[ROW_H + 16 * j:ROW_H + 16 * j + 16, :] = strips[j][0:16]
        to_down[ROW_H + 16 * j:ROW_H + 16 * j + 16, :] = strips[j][8:24]
    for i in range(10):
        to_up[ROW_I + 40 * i:ROW_I + 40 * i + 40, :] = ini_o[i]
        to_down[ROW_I + 40 * i:ROW_I + 40 * i + 40, :] = ini_o[6 + i]
    for i in range(8):
        to_up[ROW_S + 40 * i:ROW_S + 40 * i + 40, :] = src_o[i]
        to_down[ROW_S + 40 * i:ROW_S + 40 * i + 40, :] = src_o[8 + i]


def basis_body(scale, ini_x, src_x, w_main, w_strip, from_up, from_down, basis, packed,
               coef_m, coef_h, ini_v, src_v, vec_a, vec_b, sums):
    lane = lanes((8, NC))
    segment = lane // 32
    own = (1, 2, 3)
    for d in range(NH):
        for t in range(5):
            main = None
            strip = None
            parts = []
            if t < 2:
                parts.append((from_up[ROW_W + 16 * d + 8 * t:ROW_W + 16 * d + 8 * t + 8, :],
                              from_up[ROW_H + 16 * (d // 4) + 8 * t:ROW_H + 16 * (d // 4) + 8 * t + 8, :]))
            if t in own:
                parts.append((w_main[d, 8 * t - 8:8 * t, :], w_strip[d // 4, 8 * t - 8:8 * t, :]))
            if t > 2:
                s = 8 * (t - 3)
                parts.append((from_down[ROW_W + 16 * d + s:ROW_W + 16 * d + s + 8, :],
                              from_down[ROW_H + 16 * (d // 4) + s:ROW_H + 16 * (d // 4) + s + 8, :]))
            main = sum(p[0] for p in parts[1:]) + parts[0][0] if len(parts) > 1 else parts[0][0]
            strip = sum(p[1] for p in parts[1:]) + parts[0][1] if len(parts) > 1 else parts[0][1]
            strip = jnp.where(segment == d % 4, strip, 0.0)
            strip = strip + turn(strip, 32)
            strip = strip + turn(strip, 64)
            coef_m[d, 8 * t:8 * t + 8, :] = main
            coef_h[d, 8 * t:8 * t + 8, :] = strip
            dc = HALF[d][1]
            if dc != 0:
                turned = turn(main, dc)
                if dc > 0:
                    turned = jnp.where(lane < dc, turn(strip, dc - 28), turned)
                else:
                    turned = jnp.where(lane >= NC + dc, turn(strip, dc + 124), turned)
                i = TURNED_INDEX[HALF[d]]
                coef_m[i, 8 * t:8 * t + 8, :] = turned
                coef_h[i, 8 * t:8 * t + 8, :] = turn(strip, dc)

    for i in range(10):
        ini_v[i] = from_up[ROW_I + 40 * i:ROW_I + 40 * i + 40, :]
        ini_v[26 + i] = from_down[ROW_I + 40 * i:ROW_I + 40 * i + 40, :]
    for i in range(8):
        src_v[2 + i] = from_up[ROW_S + 40 * i:ROW_S + 40 * i + 40, :]
        src_v[26 + i] = from_down[ROW_S + 40 * i:ROW_S + 40 * i + 40, :]
    for i in range(NR):
        ini_v[10 + i] = ini_x[i]
        src_v[10 + i] = src_x[i]

    place = lane % 32
    inner = jnp.where((place >= 30) | (place < 2), segment, 4)
    tail = place >= 30
    head = lane < 2
    foot = lane >= NC - 2

    def image(vec, r):
        def spread(ref):
            coef = {}
            for dr in range(-2, 3):
                for dc in range(-2, 3):
                    if (dr, dc) in HALF_INDEX:
                        index = TURNED_INDEX[(dr, dc)] if dc != 0 else HALF_INDEX[(dr, dc)]
                        at = r + 15
                    else:
                        index = HALF_INDEX[(-dr, -dc)]
                        at = r + 15 + dr
                    coef[(dr, dc)] = jnp.broadcast_to(ref[index, pl.ds(at, 1), :], (8, NC))
            return coef

        def unit(coef, u):
            near = [vec[r + 10 + dr, 8 * u:8 * u + 8, :] for dr in range(-2, 3)]
            parts = []
            for dc in (-2, 2, -1, 1, 0):
                part = None
                for dr in range(-2, 3):
                    term = coef[(dr, dc)] * near[dr + 2]
                    part = term if part is None else part + term
                parts.append(turn(part, -dc))
            return ((parts[0] + parts[1]) + (parts[2] + parts[3])) + parts[4]

        coef_strip = spread(coef_h)
        strip = unit(coef_strip, 4)
        coef = spread(coef_m)
        fixed = strip
        result = []
        for g in range(4):
            main = unit(coef, g)
            edge = jnp.where(tail, turn(main, 32 * g + 28), turn(main, 32 * g + 4))
            fixed = jnp.where(inner == g, edge, fixed)
            out = jnp.where(head, turn(strip, 100 - 32 * g), main)
            result.append(jnp.where(foot, turn(strip, 124 - 32 * g), out))
        return result + [fixed]

    vectors = (vec_a, vec_b)
    for step in range(-1, STEPS):
        reach = 6 - 2 * step
        source_vec = ini_v if step < 0 else vectors[step % 2]
        target_vec = vec_a if step < 0 else vectors[(step + 1) % 2]

        def some_rows(rows, inside, step=step, source_vec=source_vec, target_vec=target_vec):
            values = []
            for r in rows:
                units = image(source_vec, r)
                olds = src_v if step < 0 else source_vec
                nexts = []
                if step + 1 < STEPS:
                    for u in range(5):
                        old = olds[r + 10, 8 * u:8 * u + 8, :]
                        nexts.append(old - units[u] if step < 0 else units[u] - 2.0 * old)
                values.append((r, units, nexts))
            for r, units, nexts in values:
                for u, value in enumerate(nexts):
                    target_vec[r + 10, 8 * u:8 * u + 8, :] = value
                if inside:
                    kept = nexts if step < 0 else units
                    for u in range(4):
                        at = 32 + 32 * step + 8 * u
                        basis[r, at:at + 8, :] = kept[u]

        def outer(i, carry, reach=reach, some_rows=some_rows):
            top = 2 * i - reach
            bottom = NR + 2 * i
            some_rows((top, top + 1, bottom, bottom + 1), False)
            return carry

        def middle(i, carry, some_rows=some_rows):
            some_rows(tuple(4 * i + j for j in range(4)), True)
            return carry

        if reach > 0:
            lax.fori_loop(0, reach // 2, outer, 0)
        lax.fori_loop(0, NR // 4, middle, 0)

    sums[...] = jnp.zeros(sums.shape, F32)

    def product(i, carry):
        total = None
        for j in range(2):
            r = 4 * i + 2 * j
            high, mid, low = split(jnp.concatenate([basis[r], basis[r + 1]], axis=1))
            left = [jnp.concatenate([x[0:32], x[96:160]], axis=0) for x in (high, mid, low)]
            both = jnp.concatenate([high[32:], mid[32:]], axis=0)
            hh = matmul_t(left[0], both)
            mm = matmul_t(left[1], both)
            rest = matmul_t(left[2], high[32:]) + matmul_t(left[0], low[32:])
            part = ((rest + mm[:, NC:]) + (hh[:, NC:] + mm[:, :NC])) + hh[:, :NC]
            total = part if total is None else total + part
        sums[...] += total
        return carry

    lax.fori_loop(0, NR // 4, product, 0)
    lane = lanes((32, NC))
    low_half = sums[0:32, :] * scale
    high_half = jnp.where(lane < 64, turn(sums[32:64, :], -32), sums[64:96, :]) * scale
    row = lax.broadcasted_iota(jnp.int32, (32, NC), 0)
    within = lane % 32
    packed[0:32, :] = jnp.where(within >= row, low_half, high_half)
    diagonal = jnp.sum(jnp.where(within == row, high_half, 0.0), axis=0, keepdims=True)
    packed[32:40, :] = jnp.broadcast_to(diagonal, (8, NC))


def split(value):
    high = value.astype(jnp.bfloat16)
    value = value - high.astype(F32)
    mid = value.astype(jnp.bfloat16)
    return high, mid, (value - mid.astype(F32)).astype(jnp.bfloat16)


def matmul_t(a, b):
    return lax.dot_general(a, b, (((1,), (1,)), ((), ())), preferred_element_type=F32)


def matmul(a, b):
    return lax.dot_general(a, b, (((1,), (0,)), ((), ())), preferred_element_type=F32)


def exact_matmul(a, b):
    return lax.dot_general(a, b, (((1,), (0,)), ((), ())), precision=lax.Precision.HIGHEST,
                           preferred_element_type=F32)


def solve_body(parts, basis, out, upper, raw):
    total = parts[0]
    for i in range(1, parts.shape[0]):
        total = total + parts[i]
    half = total[0:32]
    lane = lanes((32, NC))
    row = lax.broadcasted_iota(jnp.int32, (32, NC), 0)
    within = lane % 32
    block = lane // 32
    flipped = jnp.transpose(jnp.concatenate([half] * 4, axis=0))
    mirror = flipped[0:32]
    for b in range(1, 4):
        mirror = jnp.where(block == b, flipped[32 * b:32 * b + 32], mirror)
    project = jnp.where(within >= row, half, mirror)
    later = jnp.where(within < row, half, jnp.where(within > row, mirror, jnp.broadcast_to(total[32:33], (32, NC))))
    early = project + 2.0 * turn(project, 32)
    gram = [
        jnp.where(block == 3, turn(later, -32), turn(early, -32)),
        jnp.where(block < 2, turn(early, 64), turn(later, 64)),
        jnp.where(block < 1, turn(early, 32), turn(later, 32)),
        later,
    ]
    right = [jnp.where(lane < 32, turn(project, -32 * b), 0.0) for b in range(4)]
    g = [gram[t // 4][8 * (t % 4):8 * (t % 4) + 8] for t in range(16)]
    p = [right[t // 4][8 * (t % 4):8 * (t % 4) + 8] for t in range(16)]
    lane = lanes((8, NC))
    sub = lax.broadcasted_iota(jnp.int32, (8, NC), 0)

    def panel(first):
        for k in range(8 * first, 8 * first + 64):
            t, j = divmod(k, 8)
            cols = {i: jnp.broadcast_to(g[i][:, k:k + 1], (8, NC)) for i in range(first, first + 8)}
            inverse = 1.0 / jnp.broadcast_to(cols[t][j:j + 1, :], (8, NC))
            raw[k:k + 1, :] = g[t][j:j + 1, :]
            u = jnp.broadcast_to(g[t][j:j + 1, :], (8, NC)) * inverse
            up = jnp.broadcast_to(p[t][j:j + 1, :], (8, NC)) * inverse
            cols[t] = jnp.where(sub == j, 0.0, cols[t])
            for i in range(first, first + 8):
                g[i] = g[i] - cols[i] * u
                p[i] = p[i] - cols[i] * up
        for t in range(first, first + 8):
            line = raw[8 * t:8 * t + 8, :]
            diagonal = jnp.sum(jnp.where(lane == sub + 8 * t, line, 0.0), axis=1, keepdims=True)
            diagonal = jnp.broadcast_to(diagonal, (8, NC))
            upper[8 * t:8 * t + 8, :] = jnp.where(lane >= sub + 8 * t, line / jnp.sqrt(diagonal), 0.0)
            inverse = 1.0 / diagonal
            g[t] = g[t] * inverse
            p[t] = p[t] * inverse

    below = jnp.concatenate(g[8:16], axis=0)[:, 0:64]
    panel(0)
    scaled = jnp.concatenate([jnp.concatenate(g[0:8], axis=0), jnp.concatenate(p[0:8], axis=0)], axis=1)
    update = exact_matmul(below, scaled)
    for t in range(8, 16):
        g[t] = g[t] - update[8 * t - 64:8 * t - 56, 0:NC]
        p[t] = p[t] - update[8 * t - 64:8 * t - 56, NC:]
    panel(8)
    last = jnp.concatenate(p[8:16], axis=0)
    above = turn(scaled[:, 0:NC], 64)[:, 0:64]
    first = scaled[:, NC:] - exact_matmul(above, last)
    weights = jnp.transpose(jnp.concatenate([first, last], axis=0))[0:32]
    high, mid, low = split(weights)
    left_a = jnp.concatenate([jnp.concatenate([high, high], axis=1), jnp.concatenate([mid, mid], axis=1)], axis=0)
    left_b = jnp.concatenate([high, low], axis=1)
    for r in range(0, NR, 2):
        w_high, w_mid, w_low = split(jnp.concatenate([basis[r, 32:160, :], basis[r + 1, 32:160, :]], axis=1))
        moved_a = matmul(left_a, jnp.concatenate([w_high, w_mid], axis=0))
        moved_b = matmul(left_b, jnp.concatenate([w_low, w_high], axis=0))
        moved = moved_a[0:32] + (moved_a[32:64] + moved_b)
        out[pl.ds(r, 32, stride=NR), :] = basis[r, 0:32, :] - moved[:, :NC]
        out[pl.ds(r + 1, 32, stride=NR), :] = basis[r + 1, 0:32, :] - moved[:, NC:]


def shape(*dims):
    return jax.ShapeDtypeStruct(dims, F32)


def neighbours(count, step):
    return [(i, i + step) for i in range(count) if 0 <= i + step < count]


def on_device(dom, sub, dom_count, sub_count, reduce_groups, source, initial, lumped_mass, node_slots, stiffness):
    rows_total, cols_total = dom_count * NR, sub_count * NC
    pos = jnp.stack([lax.axis_index(dom), lax.axis_index(sub)]).astype(jnp.int32)

    def prepare(*refs):
        prepare_body(rows_total, cols_total, *refs)

    ini_x, src_x, w_main, w_strip, to_left, to_right = call(
        prepare,
        (shape(NR, 40, NC), shape(NR, 40, NC), shape(NH, 24, NC), shape(4, 24, NC), shape(176, NC), shape(176, NC)),
        scratch=[pltpu.VMEM((3, NH, 24, NC), F32)],
        in_specs=[pl.BlockSpec(memory_space=pltpu.SMEM)] + vmem_specs(5),
        out_specs=tuple(vmem_specs(6)),
        name="prepare",
    )(pos, source.reshape(NF * NR, NC), initial.reshape(NF * NR, NC), lumped_mass, node_slots,
      stiffness.reshape(36, NR, NC))
    from_right = lax.ppermute(to_left, sub, neighbours(sub_count, -1))
    from_left = lax.ppermute(to_right, sub, neighbours(sub_count, 1))
    ini_x, src_x, w_main, w_strip, to_up, to_down = call(
        columns_body,
        (shape(NR, 40, NC), shape(NR, 40, NC), shape(NH, 24, NC), shape(4, 24, NC), shape(ROW_END, NC),
         shape(ROW_END, NC)),
        name="columns",
    )(ini_x, src_x, w_main, w_strip, from_left, from_right)
    from_down = lax.ppermute(to_up, dom, neighbours(dom_count, -1))
    from_up = lax.ppermute(to_down, dom, neighbours(dom_count, 1))

    def products(*refs):
        basis_body(1.0 / float(rows_total * cols_total), *refs)

    basis, packed = call(
        products,
        (shape(NR, 160, NC), shape(40, NC)),
        scratch=[
            pltpu.VMEM((NCOEF, 40, NC), F32),
            pltpu.VMEM((NCOEF, 40, NC), F32),
            pltpu.VMEM((36, 40, NC), F32),
            pltpu.VMEM((36, 40, NC), F32),
            pltpu.VMEM((36, 40, NC), F32),
            pltpu.VMEM((36, 40, NC), F32),
            pltpu.VMEM((96, NC), F32),
        ],
        name="products",
    )(ini_x, src_x, w_main, w_strip, from_up, from_down)
    for i, (axes, count) in enumerate(reduce_groups):
        if count == 2:
            gathered = jnp.stack([packed, lax.ppermute(packed, axes, [(0, 1), (1, 0)])])
        else:
            gathered = lax.all_to_all(jnp.broadcast_to(packed[None], (count, 40, NC)), axes, 0, 0)
        if i + 1 < len(reduce_groups):
            packed = jnp.sum(gathered, axis=0)
    new_residual, upper = call(
        solve_body,
        (shape(NF * NR, NC), shape(128, 128)),
        scratch=[pltpu.VMEM((128, NC), F32)],
        name="solve",
    )(gathered, basis)
    return (new_residual.reshape(NF, NR, NC), upper)


def solution(mesh):
    dom_count, sub_count = mesh.shape["dom"], mesh.shape["sub"]
    if dom_count == 64 and sub_count == 4:
        fine = Mesh(mesh.devices.reshape(8, 4, 2, 4), ("z", "x", "c", "sub"))
        dom = ("z", "x", "c")
        groups = ((("c",), 2), (("x", "sub"), 16), (("z",), 8))
    else:
        fine, dom = mesh, ("dom",)
        groups = (("sub", sub_count), ("dom", dom_count))

    def body(*args):
        return on_device(dom, "sub", dom_count, sub_count, groups, *args)

    return jax.shard_map(
        body,
        mesh=fine,
        in_specs=(
            P(None, dom, "sub"),
            P(None, dom, "sub"),
            P(dom, "sub"),
            P(None, dom, "sub"),
            P(None, None, dom, "sub"),
        ),
        out_specs=(P(None, dom, "sub"), P()),
        check_vma=False,
    )
```

```python
import jax
import jax.numpy as jnp
import numpy as np
from jax import lax
from jax.experimental import pallas as pl
from jax.experimental.pallas import tpu as pltpu
from jax.sharding import Mesh, PartitionSpec as P

STEPS = 4
NF = 32
NR = 16
NC = 128
HALO = 10
INTERPRET = False
F32 = jnp.float32

HALF = [(0, 0), (0, 1), (0, 2)] + [(dr, dc) for dr in (1, 2) for dc in range(-2, 3)]
HALF_INDEX = {d: i for i, d in enumerate(HALF)}
NH = len(HALF)
TURNED = [d for d in HALF if d[1] != 0]
TURNED_INDEX = {d: NH + i for i, d in enumerate(TURNED)}
NCOEF = NH + len(TURNED)


def lanes(shape):
    return lax.broadcasted_iota(jnp.int32, shape, len(shape) - 1)


def turn(value, shift):
    shift = shift % NC
    return value if shift == 0 else pltpu.roll(value, shift, value.ndim - 1)


def call(body, outs, scratch=(), **kw):
    return pl.pallas_call(
        body,
        out_shape=outs,
        scratch_shapes=scratch,
        interpret=INTERPRET,
        compiler_params=pltpu.CompilerParams(vmem_limit_bytes=16 << 20),
        **kw,
    )


def near(*values):
    if INTERPRET:
        return values
    return tuple(pltpu.with_memory_space_constraint(v, pltpu.VMEM) for v in values)


def prepare_body(dom, sub_axis, rows_total, cols_total, source, initial, mass, slots, stiffness,
                 ini_x, src_x, w_main, w_strip, to_left, to_right, acc):
    row = lax.broadcasted_iota(jnp.int32, (NR, NC), 0) + lax.axis_index(dom) * NR
    col = lanes((NR, NC)) + lax.axis_index(sub_axis) * NC
    top, bottom = row == 0, row == rows_total - 1
    west, east = col == 0, col == cols_total - 1
    kept = []
    for a in range(6):
        slot = slots[a]
        in_west = (slot == 0) | (slot == 3) | (slot == 6)
        in_east = (slot == 2) | (slot == 5) | (slot == 8)
        outside = (top & (slot < 3)) | (bottom & (slot > 5)) | (west & in_west) | (east & in_east)
        kept.append(jnp.where(outside, 99, slot))
    acc[...] = jnp.zeros(acc.shape, F32)
    zero = jnp.zeros((NR, NC), F32)
    for q in range(9):
        middle = []
        for a in range(6):
            value = zero
            for b in range(6):
                value = jnp.where(kept[b] == q, stiffness[a * 6 + b], value)
            middle.append(value)
        for p in range(q + 1):
            value = zero
            for a in range(6):
                value = jnp.where(kept[a] == p, middle[a], value)
            place = HALF_INDEX[(q // 3 - p // 3, q % 3 - p % 3)]
            start = 7 + p // 3 - 1
            acc[p % 3, place, start:start + NR, :] += value
    acc[1, 0, 7:7 + NR, :] += mass[...]

    lane = lanes((24, NC))
    pack_left = [jnp.zeros((24, NC), F32) for _ in range(2)]
    pack_right = [jnp.zeros((24, NC), F32) for _ in range(2)]
    strips = [jnp.zeros((24, NC), F32) for _ in range(4)]
    for d in range(NH):
        east_turn = turn(acc[2, d], 1)
        west_turn = turn(acc[0, d], -1)
        over_east = jnp.where(lane == 0, east_turn, 0.0)
        over_west = jnp.where(lane == NC - 1, west_turn, 0.0)
        main = acc[1, d] + (east_turn - over_east) + (west_turn - over_west)
        w_main[d] = main
        own = turn(jnp.where(lane < 4, main, 0.0) + over_west, 28)
        own = own + turn(jnp.where(lane >= 124, main, 0.0) + over_east, 4)
        strips[d // 4] = strips[d // 4] + turn(own, 32 * (d % 4))
        k = 16 * (d % 8)
        pack_right[d // 8] = pack_right[d // 8] + turn(jnp.where(lane >= 118, main, 0.0) + over_east, 12 + k)
        pack_left[d // 8] = pack_left[d // 8] + turn(jnp.where(lane < 10, main, 0.0) + over_west, 4 + k)
    for j in range(4):
        w_strip[j] = strips[j]
    for j in range(2):
        to_right[128 + 24 * j:152 + 24 * j, :] = pack_right[j]
        to_left[128 + 24 * j:152 + 24 * j, :] = pack_left[j]

    lane = lanes((8, NC))
    place = lane % 32
    segment = lane // 32
    for r in range(NR):
        right = jnp.zeros((8, NC), F32)
        left = jnp.zeros((8, NC), F32)
        strip_i = jnp.zeros((8, NC), F32)
        strip_s = jnp.zeros((8, NC), F32)
        for g in range(4):
            here = segment == g
            ini = initial[pl.ds(g * 128 + r, 8, stride=NR), :]
            src = source[pl.ds(g * 128 + r, 8, stride=NR), :]
            ini_x[r, 8 * g:8 * g + 8, :] = ini
            src_x[r, 8 * g:8 * g + 8, :] = src
            turned = turn(ini, 4 + 32 * g)
            strip_i = jnp.where(here & (place < 4), turned, strip_i)
            left = jnp.where(here & (place >= 4) & (place < 14), turned, left)
            turned = turn(src, 4 + 32 * g)
            strip_s = jnp.where(here & (place < 4), turned, strip_s)
            left = jnp.where(here & (place >= 20) & (place < 30), turn(src, 20 + 32 * g), left)
            turned = turn(ini, 28 + 32 * g)
            strip_i = jnp.where(here & (place >= 28), turned, strip_i)
            turned = turn(src, 28 + 32 * g)
            strip_s = jnp.where(here & (place >= 28), turned, strip_s)
            right = jnp.where(here & (place >= 18) & (place < 28), turned, right)
            right = jnp.where(here & (place >= 2) & (place < 12), turn(ini, 12 + 32 * g), right)
        ini_x[r, 32:40, :] = strip_i
        src_x[r, 32:40, :] = strip_s
        to_right[8 * r:8 * r + 8, :] = right
        to_left[8 * r:8 * r + 8, :] = left


ROW_I = 0
ROW_S = 10 * 40
ROW_W = ROW_S + 8 * 40
ROW_H = ROW_W + NH * 16
ROW_END = ROW_H + 4 * 16


def columns_body(ini_x, src_x, w_main, w_strip, from_left, from_right,
                 ini_o, src_o, main_o, strip_o, to_up, to_down):
    lane = lanes((8, NC))
    place = lane % 32
    is_left = (place >= 18) & (place < 28)
    is_right = (place >= 4) & (place < 14)
    for r in range(NR):
        left = from_left[8 * r:8 * r + 8, :]
        right = from_right[8 * r:8 * r + 8, :]
        ini_o[r, 0:32, :] = ini_x[r, 0:32, :]
        src_o[r, 0:32, :] = src_x[r, 0:32, :]
        ini_o[r, 32:40, :] = jnp.where(is_left, turn(left, 16), jnp.where(is_right, right, ini_x[r, 32:40, :]))
        src_o[r, 32:40, :] = jnp.where(is_left, left, jnp.where(is_right, turn(right, -16), src_x[r, 32:40, :]))
    lane = lanes((24, NC))
    strips = [w_strip[j] for j in range(4)]
    for d in range(NH):
        k = 16 * (d % 8)
        left = from_left[128 + 24 * (d // 8):152 + 24 * (d // 8), :]
        right = from_right[128 + 24 * (d // 8):152 + 24 * (d // 8), :]
        left = jnp.where((lane >= 18) & (lane <= 28), turn(left, 16 - k), 0.0)
        right = jnp.where((lane >= 3) & (lane <= 13), turn(right, -k), 0.0)
        strips[d // 4] = strips[d // 4] + turn(left + right, 32 * (d % 4))
        main = w_main[d]
        main = main + jnp.where(lane == 0, turn(left, -28), 0.0)
        main = main + jnp.where(lane == NC - 1, turn(right, 124), 0.0)
        main_o[d] = main
        to_up[ROW_W + 16 * d:ROW_W + 16 * d + 16, :] = main[0:16]
        to_down[ROW_W + 16 * d:ROW_W + 16 * d + 16, :] = main[8:24]
    for j in range(4):
        strip_o[j] = strips[j]
        to_up[ROW_H + 16 * j:ROW_H + 16 * j + 16, :] = strips[j][0:16]
        to_down[ROW_H + 16 * j:ROW_H + 16 * j + 16, :] = strips[j][8:24]
    for i in range(10):
        to_up[ROW_I + 40 * i:ROW_I + 40 * i + 40, :] = ini_o[i]
        to_down[ROW_I + 40 * i:ROW_I + 40 * i + 40, :] = ini_o[6 + i]
    for i in range(8):
        to_up[ROW_S + 40 * i:ROW_S + 40 * i + 40, :] = src_o[i]
        to_down[ROW_S + 40 * i:ROW_S + 40 * i + 40, :] = src_o[8 + i]


def basis_body(scale, ini_x, src_x, w_main, w_strip, from_up, from_down, basis, packed,
               coef_m, coef_h, ini_v, src_v, vec_a, vec_b, sums):
    lane = lanes((8, NC))
    segment = lane // 32
    own = (1, 2, 3)
    for d in range(NH):
        for t in range(5):
            main = None
            strip = None
            parts = []
            if t < 2:
                parts.append((from_up[ROW_W + 16 * d + 8 * t:ROW_W + 16 * d + 8 * t + 8, :],
                              from_up[ROW_H + 16 * (d // 4) + 8 * t:ROW_H + 16 * (d // 4) + 8 * t + 8, :]))
            if t in own:
                parts.append((w_main[d, 8 * t - 8:8 * t, :], w_strip[d // 4, 8 * t - 8:8 * t, :]))
            if t > 2:
                s = 8 * (t - 3)
                parts.append((from_down[ROW_W + 16 * d + s:ROW_W + 16 * d + s + 8, :],
                              from_down[ROW_H + 16 * (d // 4) + s:ROW_H + 16 * (d // 4) + s + 8, :]))
            main = sum(p[0] for p in parts[1:]) + parts[0][0] if len(parts) > 1 else parts[0][0]
            strip = sum(p[1] for p in parts[1:]) + parts[0][1] if len(parts) > 1 else parts[0][1]
            strip = jnp.where(segment == d % 4, strip, 0.0)
            strip = strip + turn(strip, 32)
            strip = strip + turn(strip, 64)
            coef_m[d, 8 * t:8 * t + 8, :] = main
            coef_h[d, 8 * t:8 * t + 8, :] = strip
            dc = HALF[d][1]
            if dc != 0:
                turned = turn(main, dc)
                if dc > 0:
                    turned = jnp.where(lane < dc, turn(strip, dc - 28), turned)
                else:
                    turned = jnp.where(lane >= NC + dc, turn(strip, dc + 124), turned)
                i = TURNED_INDEX[HALF[d]]
                coef_m[i, 8 * t:8 * t + 8, :] = turned
                coef_h[i, 8 * t:8 * t + 8, :] = turn(strip, dc)

    for i in range(10):
        ini_v[i] = from_up[ROW_I + 40 * i:ROW_I + 40 * i + 40, :]
        ini_v[26 + i] = from_down[ROW_I + 40 * i:ROW_I + 40 * i + 40, :]
    for i in range(8):
        src_v[2 + i] = from_up[ROW_S + 40 * i:ROW_S + 40 * i + 40, :]
        src_v[26 + i] = from_down[ROW_S + 40 * i:ROW_S + 40 * i + 40, :]
    for i in range(NR):
        ini_v[10 + i] = ini_x[i]
        src_v[10 + i] = src_x[i]

    place = lane % 32
    inner = jnp.where((place >= 30) | (place < 2), segment, 4)
    tail = place >= 30
    head = lane < 2
    foot = lane >= NC - 2

    def image(vec, r):
        def spread(ref):
            coef = {}
            for dr in range(-2, 3):
                for dc in range(-2, 3):
                    if (dr, dc) in HALF_INDEX:
                        index = TURNED_INDEX[(dr, dc)] if dc != 0 else HALF_INDEX[(dr, dc)]
                        at = r + 15
                    else:
                        index = HALF_INDEX[(-dr, -dc)]
                        at = r + 15 + dr
                    coef[(dr, dc)] = jnp.broadcast_to(ref[index, pl.ds(at, 1), :], (8, NC))
            return coef

        def unit(coef, u):
            near = [vec[r + 10 + dr, 8 * u:8 * u + 8, :] for dr in range(-2, 3)]
            parts = []
            for dc in (-2, 2, -1, 1, 0):
                part = None
                for dr in range(-2, 3):
                    term = coef[(dr, dc)] * near[dr + 2]
                    part = term if part is None else part + term
                parts.append(turn(part, -dc))
            return ((parts[0] + parts[1]) + (parts[2] + parts[3])) + parts[4]

        coef_strip = spread(coef_h)
        strip = unit(coef_strip, 4)
        coef = spread(coef_m)
        fixed = strip
        result = []
        for g in range(4):
            main = unit(coef, g)
            edge = jnp.where(tail, turn(main, 32 * g + 28), turn(main, 32 * g + 4))
            fixed = jnp.where(inner == g, edge, fixed)
            out = jnp.where(head, turn(strip, 100 - 32 * g), main)
            result.append(jnp.where(foot, turn(strip, 124 - 32 * g), out))
        return result + [fixed]

    vectors = (vec_a, vec_b)
    for step in range(-1, STEPS):
        reach = 6 - 2 * step
        source_vec = ini_v if step < 0 else vectors[step % 2]
        target_vec = vec_a if step < 0 else vectors[(step + 1) % 2]

        def some_rows(rows, inside, step=step, source_vec=source_vec, target_vec=target_vec):
            values = []
            for r in rows:
                units = image(source_vec, r)
                olds = src_v if step < 0 else source_vec
                nexts = []
                if step + 1 < STEPS:
                    for u in range(5):
                        old = olds[r + 10, 8 * u:8 * u + 8, :]
                        nexts.append(old - units[u] if step < 0 else units[u] - 2.0 * old)
                values.append((r, units, nexts))
            for r, units, nexts in values:
                for u, value in enumerate(nexts):
                    target_vec[r + 10, 8 * u:8 * u + 8, :] = value
                if inside:
                    kept = nexts if step < 0 else units
                    for u in range(4):
                        at = 32 + 32 * step + 8 * u
                        basis[r, at:at + 8, :] = kept[u]

        def outer(i, carry, reach=reach, some_rows=some_rows):
            top = 2 * i - reach
            bottom = NR + 2 * i
            some_rows((top, top + 1, bottom, bottom + 1), False)
            return carry

        def middle(i, carry, some_rows=some_rows):
            some_rows(tuple(4 * i + j for j in range(4)), True)
            return carry

        if reach > 0:
            lax.fori_loop(0, reach // 2, outer, 0)
        lax.fori_loop(0, NR // 4, middle, 0)

    sums[...] = jnp.zeros(sums.shape, F32)

    def product(i, carry):
        total = None
        for j in range(2):
            r = 4 * i + 2 * j
            high, mid, low = split(jnp.concatenate([basis[r], basis[r + 1]], axis=1))
            left = [jnp.concatenate([x[0:32], x[96:160]], axis=0) for x in (high, mid, low)]
            both = jnp.concatenate([high[32:], mid[32:]], axis=0)
            hh = matmul_t(left[0], both)
            mm = matmul_t(left[1], both)
            rest = matmul_t(left[2], high[32:]) + matmul_t(left[0], low[32:])
            part = ((rest + mm[:, NC:]) + (hh[:, NC:] + mm[:, :NC])) + hh[:, :NC]
            total = part if total is None else total + part
        sums[...] += total
        return carry

    lax.fori_loop(0, NR // 4, product, 0)
    lane = lanes((32, NC))
    low_half = sums[0:32, :] * scale
    high_half = jnp.where(lane < 64, turn(sums[32:64, :], -32), sums[64:96, :]) * scale
    row = lax.broadcasted_iota(jnp.int32, (32, NC), 0)
    within = lane % 32
    packed[0:32, :] = jnp.where(within >= row, low_half, high_half)
    diagonal = jnp.sum(jnp.where(within == row, high_half, 0.0), axis=0, keepdims=True)
    packed[32:40, :] = jnp.broadcast_to(diagonal, (8, NC))


def split(value):
    high = value.astype(jnp.bfloat16)
    value = value - high.astype(F32)
    mid = value.astype(jnp.bfloat16)
    return high, mid, (value - mid.astype(F32)).astype(jnp.bfloat16)


def matmul_t(a, b):
    return lax.dot_general(a, b, (((1,), (1,)), ((), ())), preferred_element_type=F32)


def matmul(a, b):
    return lax.dot_general(a, b, (((1,), (0,)), ((), ())), preferred_element_type=F32)


def exact_matmul(a, b):
    return lax.dot_general(a, b, (((1,), (0,)), ((), ())), precision=lax.Precision.HIGHEST,
                           preferred_element_type=F32)


def solve_body(parts, basis, out, upper, raw):
    total = parts[0]
    for i in range(1, parts.shape[0]):
        total = total + parts[i]
    half = total[0:32]
    lane = lanes((32, NC))
    row = lax.broadcasted_iota(jnp.int32, (32, NC), 0)
    within = lane % 32
    block = lane // 32
    flipped = jnp.transpose(jnp.concatenate([half] * 4, axis=0))
    mirror = flipped[0:32]
    for b in range(1, 4):
        mirror = jnp.where(block == b, flipped[32 * b:32 * b + 32], mirror)
    project = jnp.where(within >= row, half, mirror)
    later = jnp.where(within < row, half, jnp.where(within > row, mirror, jnp.broadcast_to(total[32:33], (32, NC))))
    early = project + 2.0 * turn(project, 32)
    gram = [
        jnp.where(block == 3, turn(later, -32), turn(early, -32)),
        jnp.where(block < 2, turn(early, 64), turn(later, 64)),
        jnp.where(block < 1, turn(early, 32), turn(later, 32)),
        later,
    ]
    right = [jnp.where(lane < 32, turn(project, -32 * b), 0.0) for b in range(4)]
    g = [gram[t // 4][8 * (t % 4):8 * (t % 4) + 8] for t in range(16)]
    p = [right[t // 4][8 * (t % 4):8 * (t % 4) + 8] for t in range(16)]
    lane = lanes((8, NC))
    sub = lax.broadcasted_iota(jnp.int32, (8, NC), 0)

    def spread(value, j):
        return jnp.broadcast_to(value[j:j + 1, :], (8, NC))

    def columns(value, base):
        return [jnp.broadcast_to(value[:, base + q:base + q + 1], (8, NC)) for q in range(8)]

    def panel(first):
        for t in range(first, first + 8):
            col = columns(g[t], 8 * t)
            steps = []
            for j in range(8):
                inverse = 1.0 / spread(col[j], j)
                raw[8 * t + j:8 * t + j + 1, :] = g[t][j:j + 1, :]
                u = spread(g[t], j) * inverse
                up = spread(p[t], j) * inverse
                m = jnp.where(sub == j, 0.0, col[j])
                scaled_cols = {}
                for q in range(j + 1, 8):
                    scaled_cols[q] = spread(col[q], j) * inverse
                    col[q] = col[q] - m * scaled_cols[q]
                g[t] = g[t] - m * u
                p[t] = p[t] - m * up
                steps.append((scaled_cols, u, up))
            for i in [first + (t - first + n) % 8 for n in range(1, 8)]:
                col = columns(g[i], 8 * t)
                for j in range(8):
                    scaled_cols, u, up = steps[j]
                    for q in range(j + 1, 8):
                        col[q] = col[q] - col[j] * scaled_cols[q]
                    g[i] = g[i] - col[j] * u
                    p[i] = p[i] - col[j] * up
        for t in range(first, first + 8):
            line = raw[8 * t:8 * t + 8, :]
            diagonal = jnp.sum(jnp.where(lane == sub + 8 * t, line, 0.0), axis=1, keepdims=True)
            diagonal = jnp.broadcast_to(diagonal, (8, NC))
            upper[8 * t:8 * t + 8, :] = jnp.where(lane >= sub + 8 * t, line / jnp.sqrt(diagonal), 0.0)
            inverse = 1.0 / diagonal
            g[t] = g[t] * inverse
            p[t] = p[t] * inverse

    below = jnp.concatenate(g[8:16], axis=0)[:, 0:64]
    panel(0)
    scaled = jnp.concatenate([jnp.concatenate(g[0:8], axis=0), jnp.concatenate(p[0:8], axis=0)], axis=1)
    update = exact_matmul(below, scaled)
    for t in range(8, 16):
        g[t] = g[t] - update[8 * t - 64:8 * t - 56, 0:NC]
        p[t] = p[t] - update[8 * t - 64:8 * t - 56, NC:]
    panel(8)
    last = jnp.concatenate(p[8:16], axis=0)
    above = turn(scaled[:, 0:NC], 64)[:, 0:64]
    first = scaled[:, NC:] - exact_matmul(above, last)
    weights = jnp.transpose(jnp.concatenate([first, last], axis=0))[0:32]
    high, mid, low = split(weights)
    left_a = jnp.concatenate([jnp.concatenate([high, high], axis=1), jnp.concatenate([mid, mid], axis=1)], axis=0)
    left_b = jnp.concatenate([high, low], axis=1)
    for r in range(0, NR, 2):
        w_high, w_mid, w_low = split(jnp.concatenate([basis[r, 32:160, :], basis[r + 1, 32:160, :]], axis=1))
        moved_a = matmul(left_a, jnp.concatenate([w_high, w_mid], axis=0))
        moved_b = matmul(left_b, jnp.concatenate([w_low, w_high], axis=0))
        moved = moved_a[0:32] + (moved_a[32:64] + moved_b)
        out[pl.ds(r, 32, stride=NR), :] = basis[r, 0:32, :] - moved[:, :NC]
        out[pl.ds(r + 1, 32, stride=NR), :] = basis[r + 1, 0:32, :] - moved[:, NC:]


def far(*dims):
    return jax.ShapeDtypeStruct(dims, F32)


def shape(*dims):
    return far(*dims) if INTERPRET else pltpu.VMEM(dims, F32)


def neighbours(count, step):
    return [(i, i + step) for i in range(count) if 0 <= i + step < count]


def on_device(dom, sub, dom_count, sub_count, reduce_groups, source, initial, lumped_mass, node_slots, stiffness):
    rows_total, cols_total = dom_count * NR, sub_count * NC

    def prepare(*refs):
        prepare_body(dom, sub, rows_total, cols_total, *refs)

    ini_x, src_x, w_main, w_strip, to_left, to_right = call(
        prepare,
        (shape(NR, 40, NC), shape(NR, 40, NC), shape(NH, 24, NC), shape(4, 24, NC), shape(176, NC), shape(176, NC)),
        scratch=[pltpu.VMEM((3, NH, 24, NC), F32)],
        name="prepare",
    )(source.reshape(NF * NR, NC), initial.reshape(NF * NR, NC), lumped_mass, node_slots,
      stiffness.reshape(36, NR, NC))
    from_right = lax.ppermute(to_left, sub, neighbours(sub_count, -1))
    from_left = lax.ppermute(to_right, sub, neighbours(sub_count, 1))
    ini_x, src_x, w_main, w_strip, to_up, to_down = call(
        columns_body,
        (shape(NR, 40, NC), shape(NR, 40, NC), shape(NH, 24, NC), shape(4, 24, NC), shape(ROW_END, NC),
         shape(ROW_END, NC)),
        name="columns",
    )(*near(ini_x, src_x, w_main, w_strip, from_left, from_right))
    from_down = lax.ppermute(to_up, dom, neighbours(dom_count, -1))
    from_up = lax.ppermute(to_down, dom, neighbours(dom_count, 1))

    def products(*refs):
        basis_body(1.0 / float(rows_total * cols_total), *refs)

    basis, packed = call(
        products,
        (shape(NR, 160, NC), shape(40, NC)),
        scratch=[
            pltpu.VMEM((NCOEF, 40, NC), F32),
            pltpu.VMEM((NCOEF, 40, NC), F32),
            pltpu.VMEM((36, 40, NC), F32),
            pltpu.VMEM((36, 40, NC), F32),
            pltpu.VMEM((36, 40, NC), F32),
            pltpu.VMEM((36, 40, NC), F32),
            pltpu.VMEM((96, NC), F32),
        ],
        name="products",
    )(*near(ini_x, src_x, w_main, w_strip, from_up, from_down))
    for i, (axes, count) in enumerate(reduce_groups):
        if count == 2:
            gathered = jnp.stack([packed, lax.ppermute(packed, axes, [(0, 1), (1, 0)])])
        else:
            gathered = lax.all_to_all(jnp.broadcast_to(packed[None], (count, 40, NC)), axes, 0, 0)
        if i + 1 < len(reduce_groups):
            packed = jnp.sum(gathered, axis=0)
    new_residual, upper = call(
        solve_body,
        (far(NF * NR, NC), far(128, 128)),
        scratch=[pltpu.VMEM((128, NC), F32)],
        name="solve",
    )(*near(gathered, basis))
    return (new_residual.reshape(NF, NR, NC), upper)


def solution(mesh):
    dom_count, sub_count = mesh.shape["dom"], mesh.shape["sub"]
    if dom_count == 64 and sub_count == 4:
        fine = Mesh(mesh.devices.reshape(8, 4, 2, 4), ("z", "x", "c", "sub"))
        dom = ("z", "x", "c")
        groups = ((("c",), 2), (("x", "sub"), 16), (("z",), 8))
    else:
        fine, dom = mesh, ("dom",)
        groups = (("sub", sub_count), ("dom", dom_count))

    def body(*args):
        return on_device(dom, "sub", dom_count, sub_count, groups, *args)

    return jax.shard_map(
        body,
        mesh=fine,
        in_specs=(
            P(None, dom, "sub"),
            P(None, dom, "sub"),
            P(dom, "sub"),
            P(None, dom, "sub"),
            P(None, None, dom, "sub"),
        ),
        out_specs=(P(None, dom, "sub"), P()),
        check_vma=False,
    )
```

```python
import jax
import jax.numpy as jnp
import numpy as np
from jax import lax
from jax.experimental import pallas as pl
from jax.experimental.pallas import tpu as pltpu
from jax.sharding import Mesh, PartitionSpec as P

STEPS = 4
NF = 32
NR = 16
NC = 128
HALO = 10
INTERPRET = False
F32 = jnp.float32

HALF = [(0, 0), (0, 1), (0, 2)] + [(dr, dc) for dr in (1, 2) for dc in range(-2, 3)]
HALF_INDEX = {d: i for i, d in enumerate(HALF)}
NH = len(HALF)
TURNED = [d for d in HALF if d[1] != 0]
TURNED_INDEX = {d: NH + i for i, d in enumerate(TURNED)}
NCOEF = NH + len(TURNED)


def lanes(shape):
    return lax.broadcasted_iota(jnp.int32, shape, len(shape) - 1)


def turn(value, shift):
    shift = shift % NC
    return value if shift == 0 else pltpu.roll(value, shift, value.ndim - 1)


def call(body, outs, scratch=(), **kw):
    return pl.pallas_call(
        body,
        out_shape=outs,
        scratch_shapes=scratch,
        interpret=INTERPRET,
        compiler_params=pltpu.CompilerParams(vmem_limit_bytes=16 << 20),
        **kw,
    )


def near(*values):
    if INTERPRET:
        return values
    return tuple(pltpu.with_memory_space_constraint(v, pltpu.VMEM) for v in values)


def distant(*values):
    if INTERPRET:
        return values
    return tuple(pltpu.with_memory_space_constraint(v, pltpu.HBM) for v in values)


MAIN_I = 0
MAIN_S = 10 * 32
MAIN_W = MAIN_S + 8 * 32
MAIN_END = MAIN_W + NH * 16
STRIP_I = 0
STRIP_S = 10 * 8
STRIP_W = STRIP_S + 8 * 8
STRIP_END = STRIP_W + 4 * 16


def prepare_body(dom, sub_axis, rows_total, cols_total, source_far, initial_far, mass_far, slots_far, stiffness_far,
                 ini_m, src_m, ini_h, src_h, w_main, w_strip, to_left, to_right, to_up, to_down,
                 acc, source, initial, mass, slots, stiffness, arrived):
    copies = [
        pltpu.make_async_copy(far_ref, near_ref, arrived.at[i])
        for i, (far_ref, near_ref) in enumerate((
            (slots_far, slots), (stiffness_far, stiffness), (mass_far, mass), (initial_far, initial),
            (source_far, source)))
    ]
    for copy in copies:
        copy.start()
    for copy in copies[:3]:
        copy.wait()
    row = lax.broadcasted_iota(jnp.int32, (NR, NC), 0) + lax.axis_index(dom) * NR
    col = lanes((NR, NC)) + lax.axis_index(sub_axis) * NC
    top, bottom = row == 0, row == rows_total - 1
    west, east = col == 0, col == cols_total - 1
    kept = []
    for a in range(6):
        slot = slots[a]
        in_west = (slot == 0) | (slot == 3) | (slot == 6)
        in_east = (slot == 2) | (slot == 5) | (slot == 8)
        outside = (top & (slot < 3)) | (bottom & (slot > 5)) | (west & in_west) | (east & in_east)
        kept.append(jnp.where(outside, 99, slot))
    acc[...] = jnp.zeros(acc.shape, F32)
    zero = jnp.zeros((NR, NC), F32)
    for q in range(9):
        middle = []
        for a in range(6):
            value = zero
            for b in range(6):
                value = jnp.where(kept[b] == q, stiffness[a * 6 + b], value)
            middle.append(value)
        for p in range(q + 1):
            value = zero
            for a in range(6):
                value = jnp.where(kept[a] == p, middle[a], value)
            place = HALF_INDEX[(q // 3 - p // 3, q % 3 - p % 3)]
            start = 7 + p // 3 - 1
            acc[p % 3, place, start:start + NR, :] += value
    acc[1, 0, 7:7 + NR, :] += mass[...]

    lane = lanes((24, NC))
    pack_left = [jnp.zeros((24, NC), F32) for _ in range(2)]
    pack_right = [jnp.zeros((24, NC), F32) for _ in range(2)]
    strips = [jnp.zeros((24, NC), F32) for _ in range(4)]
    for d in range(NH):
        east_turn = turn(acc[2, d], 1)
        west_turn = turn(acc[0, d], -1)
        over_east = jnp.where(lane == 0, east_turn, 0.0)
        over_west = jnp.where(lane == NC - 1, west_turn, 0.0)
        main = acc[1, d] + (east_turn - over_east) + (west_turn - over_west)
        w_main[d] = main
        to_up[MAIN_W + 16 * d:MAIN_W + 16 * d + 16, :] = main[0:16]
        to_down[MAIN_W + 16 * d:MAIN_W + 16 * d + 16, :] = main[8:24]
        own = turn(jnp.where(lane < 4, main, 0.0) + over_west, 28)
        own = own + turn(jnp.where(lane >= 124, main, 0.0) + over_east, 4)
        strips[d // 4] = strips[d // 4] + turn(own, 32 * (d % 4))
        k = 16 * (d % 8)
        pack_right[d // 8] = pack_right[d // 8] + turn(jnp.where(lane >= 118, main, 0.0) + over_east, 12 + k)
        pack_left[d // 8] = pack_left[d // 8] + turn(jnp.where(lane < 10, main, 0.0) + over_west, 4 + k)
    for j in range(4):
        w_strip[j] = strips[j]
    for j in range(2):
        to_right[128 + 24 * j:152 + 24 * j, :] = pack_right[j]
        to_left[128 + 24 * j:152 + 24 * j, :] = pack_left[j]

    for copy in copies[3:]:
        copy.wait()
    lane = lanes((8, NC))
    place = lane % 32
    segment = lane // 32
    for r in range(NR):
        right = jnp.zeros((8, NC), F32)
        left = jnp.zeros((8, NC), F32)
        strip_i = jnp.zeros((8, NC), F32)
        strip_s = jnp.zeros((8, NC), F32)
        for g in range(4):
            here = segment == g
            ini = initial[pl.ds(g * 128 + r, 8, stride=NR), :]
            src = source[pl.ds(g * 128 + r, 8, stride=NR), :]
            at = 8 * g
            ini_m[r, at:at + 8, :] = ini
            src_m[r, at:at + 8, :] = src
            if r < 10:
                to_up[MAIN_I + 32 * r + at:MAIN_I + 32 * r + at + 8, :] = ini
            if r >= 6:
                to_down[MAIN_I + 32 * (r - 6) + at:MAIN_I + 32 * (r - 6) + at + 8, :] = ini
            if r < 8:
                to_up[MAIN_S + 32 * r + at:MAIN_S + 32 * r + at + 8, :] = src
            else:
                to_down[MAIN_S + 32 * (r - 8) + at:MAIN_S + 32 * (r - 8) + at + 8, :] = src
            turned = turn(ini, 4 + 32 * g)
            strip_i = jnp.where(here & (place < 4), turned, strip_i)
            left = jnp.where(here & (place >= 4) & (place < 14), turned, left)
            turned = turn(src, 4 + 32 * g)
            strip_s = jnp.where(here & (place < 4), turned, strip_s)
            left = jnp.where(here & (place >= 20) & (place < 30), turn(src, 20 + 32 * g), left)
            turned = turn(ini, 28 + 32 * g)
            strip_i = jnp.where(here & (place >= 28), turned, strip_i)
            turned = turn(src, 28 + 32 * g)
            strip_s = jnp.where(here & (place >= 28), turned, strip_s)
            right = jnp.where(here & (place >= 18) & (place < 28), turned, right)
            right = jnp.where(here & (place >= 2) & (place < 12), turn(ini, 12 + 32 * g), right)
        ini_h[r] = strip_i
        src_h[r] = strip_s
        to_right[8 * r:8 * r + 8, :] = right
        to_left[8 * r:8 * r + 8, :] = left


def columns_body(sub_axis, sub_count, ini_h, src_h, w_strip, from_left, from_right, ini_o, src_o, strip_o, to_up, to_down):
    lane = lanes((8, NC))
    place = lane % 32
    is_left = (place >= 18) & (place < 28)
    is_right = (place >= 4) & (place < 14)
    at = lax.axis_index(sub_axis)
    has_left, has_right = at > 0, at < sub_count - 1
    for r in range(NR):
        left = jnp.where(has_left, from_left[8 * r:8 * r + 8, :], 0.0)
        right = jnp.where(has_right, from_right[8 * r:8 * r + 8, :], 0.0)
        ini = jnp.where(is_left, turn(left, 16), jnp.where(is_right, right, ini_h[r]))
        src = jnp.where(is_left, left, jnp.where(is_right, turn(right, -16), src_h[r]))
        ini_o[r] = ini
        src_o[r] = src
        if r < 10:
            to_up[STRIP_I + 8 * r:STRIP_I + 8 * r + 8, :] = ini
        if r >= 6:
            to_down[STRIP_I + 8 * (r - 6):STRIP_I + 8 * (r - 6) + 8, :] = ini
        if r < 8:
            to_up[STRIP_S + 8 * r:STRIP_S + 8 * r + 8, :] = src
        else:
            to_down[STRIP_S + 8 * (r - 8):STRIP_S + 8 * (r - 8) + 8, :] = src
    lane = lanes((24, NC))
    strips = [w_strip[j] for j in range(4)]
    for d in range(NH):
        k = 16 * (d % 8)
        left = from_left[128 + 24 * (d // 8):152 + 24 * (d // 8), :]
        right = from_right[128 + 24 * (d // 8):152 + 24 * (d // 8), :]
        left = jnp.where((lane >= 18) & (lane <= 28) & has_left, turn(left, 16 - k), 0.0)
        right = jnp.where((lane >= 3) & (lane <= 13) & has_right, turn(right, -k), 0.0)
        strips[d // 4] = strips[d // 4] + turn(left + right, 32 * (d % 4))
    for j in range(4):
        strip_o[j] = strips[j]
        to_up[STRIP_W + 16 * j:STRIP_W + 16 * j + 16, :] = strips[j][0:16]
        to_down[STRIP_W + 16 * j:STRIP_W + 16 * j + 16, :] = strips[j][8:24]


def basis_body(dom, dom_count, scale, ini_m, src_m, ini_h, src_h, w_main, w_strip, up_main, down_main, up_strip, down_strip,
               basis, packed,
               coef_m, coef_h, ini_v, src_v, vec_a, vec_b, sums):
    lane = lanes((8, NC))
    segment = lane // 32
    own = (1, 2, 3)
    at = lax.axis_index(dom)
    has_up, has_down = at > 0, at < dom_count - 1

    def upper(ref, start, size=8):
        return jnp.where(has_up, ref[start:start + size, :], 0.0)

    def lower(ref, start, size=8):
        return jnp.where(has_down, ref[start:start + size, :], 0.0)

    for d in range(NH):
        for t in range(5):
            main = None
            strip = None
            parts = []
            if t < 2:
                parts.append((upper(up_main, MAIN_W + 16 * d + 8 * t), upper(up_strip, STRIP_W + 16 * (d // 4) + 8 * t)))
            if t in own:
                parts.append((w_main[d, 8 * t - 8:8 * t, :], w_strip[d // 4, 8 * t - 8:8 * t, :]))
            if t > 2:
                s = 8 * (t - 3)
                parts.append((lower(down_main, MAIN_W + 16 * d + s), lower(down_strip, STRIP_W + 16 * (d // 4) + s)))
            main = sum(p[0] for p in parts[1:]) + parts[0][0] if len(parts) > 1 else parts[0][0]
            strip = sum(p[1] for p in parts[1:]) + parts[0][1] if len(parts) > 1 else parts[0][1]
            strip = jnp.where(segment == d % 4, strip, 0.0)
            strip = strip + turn(strip, 32)
            strip = strip + turn(strip, 64)
            main = jnp.where(lane == 0, turn(strip, -28), main)
            main = jnp.where(lane == NC - 1, turn(strip, 124), main)
            coef_m[d, 8 * t:8 * t + 8, :] = main
            coef_h[d, 8 * t:8 * t + 8, :] = strip
            dc = HALF[d][1]
            if dc != 0:
                turned = turn(main, dc)
                if dc > 0:
                    turned = jnp.where(lane < dc, turn(strip, dc - 28), turned)
                else:
                    turned = jnp.where(lane >= NC + dc, turn(strip, dc + 124), turned)
                i = TURNED_INDEX[HALF[d]]
                coef_m[i, 8 * t:8 * t + 8, :] = turned
                coef_h[i, 8 * t:8 * t + 8, :] = turn(strip, dc)

    for i in range(10):
        ini_v[i, 0:32] = upper(up_main, MAIN_I + 32 * i, 32)
        ini_v[i, 32:40] = upper(up_strip, STRIP_I + 8 * i)
        ini_v[26 + i, 0:32] = lower(down_main, MAIN_I + 32 * i, 32)
        ini_v[26 + i, 32:40] = lower(down_strip, STRIP_I + 8 * i)
    for i in range(8):
        src_v[2 + i, 0:32] = upper(up_main, MAIN_S + 32 * i, 32)
        src_v[2 + i, 32:40] = upper(up_strip, STRIP_S + 8 * i)
        src_v[26 + i, 0:32] = lower(down_main, MAIN_S + 32 * i, 32)
        src_v[26 + i, 32:40] = lower(down_strip, STRIP_S + 8 * i)
    for i in range(NR):
        ini_v[10 + i, 0:32] = ini_m[i]
        ini_v[10 + i, 32:40] = ini_h[i]
        src_v[10 + i, 0:32] = src_m[i]
        src_v[10 + i, 32:40] = src_h[i]

    place = lane % 32
    inner = jnp.where((place >= 30) | (place < 2), segment, 4)
    tail = place >= 30
    head = lane < 2
    foot = lane >= NC - 2

    def image(vec, r):
        def spread(ref):
            coef = {}
            for dr in range(-2, 3):
                for dc in range(-2, 3):
                    if (dr, dc) in HALF_INDEX:
                        index = TURNED_INDEX[(dr, dc)] if dc != 0 else HALF_INDEX[(dr, dc)]
                        at = r + 15
                    else:
                        index = HALF_INDEX[(-dr, -dc)]
                        at = r + 15 + dr
                    coef[(dr, dc)] = jnp.broadcast_to(ref[index, pl.ds(at, 1), :], (8, NC))
            return coef

        def unit(coef, u):
            near = [vec[r + 10 + dr, 8 * u:8 * u + 8, :] for dr in range(-2, 3)]
            parts = []
            for dc in (-2, 2, -1, 1, 0):
                part = None
                for dr in range(-2, 3):
                    term = coef[(dr, dc)] * near[dr + 2]
                    part = term if part is None else part + term
                parts.append(turn(part, -dc))
            return ((parts[0] + parts[1]) + (parts[2] + parts[3])) + parts[4]

        coef_strip = spread(coef_h)
        strip = unit(coef_strip, 4)
        coef = spread(coef_m)
        fixed = strip
        result = []
        for g in range(4):
            main = unit(coef, g)
            edge = jnp.where(tail, turn(main, 32 * g + 28), turn(main, 32 * g + 4))
            fixed = jnp.where(inner == g, edge, fixed)
            out = jnp.where(head, turn(strip, 100 - 32 * g), main)
            result.append(jnp.where(foot, turn(strip, 124 - 32 * g), out))
        return result + [fixed]

    vectors = (vec_a, vec_b)
    for step in range(-1, STEPS):
        reach = 6 - 2 * step
        source_vec = ini_v if step < 0 else vectors[step % 2]
        target_vec = vec_a if step < 0 else vectors[(step + 1) % 2]

        def some_rows(rows, inside, step=step, source_vec=source_vec, target_vec=target_vec):
            values = []
            for r in rows:
                units = image(source_vec, r)
                olds = src_v if step < 0 else source_vec
                nexts = []
                if step + 1 < STEPS:
                    for u in range(5):
                        old = olds[r + 10, 8 * u:8 * u + 8, :]
                        nexts.append(old - units[u] if step < 0 else units[u] - 2.0 * old)
                values.append((r, units, nexts))
            for r, units, nexts in values:
                for u, value in enumerate(nexts):
                    target_vec[r + 10, 8 * u:8 * u + 8, :] = value
                if inside:
                    kept = nexts if step < 0 else units
                    for u in range(4):
                        at = 32 + 32 * step + 8 * u
                        basis[r, at:at + 8, :] = kept[u]

        def outer(i, carry, reach=reach, some_rows=some_rows):
            top = 2 * i - reach
            bottom = NR + 2 * i
            some_rows((top, top + 1, bottom, bottom + 1), False)
            return carry

        def middle(i, carry, some_rows=some_rows):
            some_rows(tuple(4 * i + j for j in range(4)), True)
            return carry

        if reach > 0:
            lax.fori_loop(0, reach // 2, outer, 0)
        lax.fori_loop(0, NR // 4, middle, 0)

    sums[...] = jnp.zeros(sums.shape, F32)

    def product(i, carry):
        total = None
        for j in range(2):
            r = 4 * i + 2 * j
            high, mid, low = split(jnp.concatenate([basis[r], basis[r + 1]], axis=1))
            left = [jnp.concatenate([x[0:32], x[96:160]], axis=0) for x in (high, mid, low)]
            both = jnp.concatenate([high[32:], mid[32:]], axis=0)
            hh = matmul_t(left[0], both)
            mm = matmul_t(left[1], both)
            rest = matmul_t(left[2], high[32:]) + matmul_t(left[0], low[32:])
            part = ((rest + mm[:, NC:]) + (hh[:, NC:] + mm[:, :NC])) + hh[:, :NC]
            total = part if total is None else total + part
        sums[...] += total
        return carry

    lax.fori_loop(0, NR // 4, product, 0)
    lane = lanes((32, NC))
    low_half = sums[0:32, :] * scale
    high_half = jnp.where(lane < 64, turn(sums[32:64, :], -32), sums[64:96, :]) * scale
    row = lax.broadcasted_iota(jnp.int32, (32, NC), 0)
    within = lane % 32
    packed[0:32, :] = jnp.where(within >= row, low_half, high_half)
    diagonal = jnp.sum(jnp.where(within == row, high_half, 0.0), axis=0, keepdims=True)
    packed[32:40, :] = jnp.broadcast_to(diagonal, (8, NC))


def split(value):
    high = value.astype(jnp.bfloat16)
    value = value - high.astype(F32)
    mid = value.astype(jnp.bfloat16)
    return high, mid, (value - mid.astype(F32)).astype(jnp.bfloat16)


def matmul_t(a, b):
    return lax.dot_general(a, b, (((1,), (1,)), ((), ())), preferred_element_type=F32)


def matmul(a, b):
    return lax.dot_general(a, b, (((1,), (0,)), ((), ())), preferred_element_type=F32)


def exact_matmul(a, b):
    return lax.dot_general(a, b, (((1,), (0,)), ((), ())), precision=lax.Precision.HIGHEST,
                           preferred_element_type=F32)


def solve_body(parts, basis, out, upper, raw):
    total = parts[0]
    for i in range(1, parts.shape[0]):
        total = total + parts[i]
    half = total[0:32]
    lane = lanes((32, NC))
    row = lax.broadcasted_iota(jnp.int32, (32, NC), 0)
    within = lane % 32
    block = lane // 32
    flipped = jnp.transpose(jnp.concatenate([half] * 4, axis=0))
    mirror = flipped[0:32]
    for b in range(1, 4):
        mirror = jnp.where(block == b, flipped[32 * b:32 * b + 32], mirror)
    project = jnp.where(within >= row, half, mirror)
    later = jnp.where(within < row, half, jnp.where(within > row, mirror, jnp.broadcast_to(total[32:33], (32, NC))))
    early = project + 2.0 * turn(project, 32)
    gram = [
        jnp.where(block == 3, turn(later, -32), turn(early, -32)),
        jnp.where(block < 2, turn(early, 64), turn(later, 64)),
        jnp.where(block < 1, turn(early, 32), turn(later, 32)),
        later,
    ]
    right = [jnp.where(lane < 32, turn(project, -32 * b), 0.0) for b in range(4)]
    g = [gram[t // 4][8 * (t % 4):8 * (t % 4) + 8] for t in range(16)]
    p = [right[t // 4][8 * (t % 4):8 * (t % 4) + 8] for t in range(16)]
    lane = lanes((8, NC))
    sub = lax.broadcasted_iota(jnp.int32, (8, NC), 0)

    def spread(value, j):
        return jnp.broadcast_to(value[j:j + 1, :], (8, NC))

    def columns(value, base):
        return [jnp.broadcast_to(value[:, base + q:base + q + 1], (8, NC)) for q in range(8)]

    def panel(first):
        for t in range(first, first + 8):
            col = columns(g[t], 8 * t)
            steps = []
            for j in range(8):
                inverse = 1.0 / spread(col[j], j)
                raw[8 * t + j:8 * t + j + 1, :] = g[t][j:j + 1, :]
                u = spread(g[t], j) * inverse
                up = spread(p[t], j) * inverse
                m = jnp.where(sub == j, 0.0, col[j])
                scaled_cols = {}
                for q in range(j + 1, 8):
                    scaled_cols[q] = spread(col[q], j) * inverse
                    col[q] = col[q] - m * scaled_cols[q]
                g[t] = g[t] - m * u
                p[t] = p[t] - m * up
                steps.append((scaled_cols, u, up))
            for i in [first + (t - first + n) % 8 for n in range(1, 8)]:
                col = columns(g[i], 8 * t)
                for j in range(8):
                    scaled_cols, u, up = steps[j]
                    for q in range(j + 1, 8):
                        col[q] = col[q] - col[j] * scaled_cols[q]
                    g[i] = g[i] - col[j] * u
                    p[i] = p[i] - col[j] * up
        for t in range(first, first + 8):
            line = raw[8 * t:8 * t + 8, :]
            diagonal = jnp.sum(jnp.where(lane == sub + 8 * t, line, 0.0), axis=1, keepdims=True)
            diagonal = jnp.broadcast_to(diagonal, (8, NC))
            upper[8 * t:8 * t + 8, :] = jnp.where(lane >= sub + 8 * t, line / jnp.sqrt(diagonal), 0.0)
            inverse = 1.0 / diagonal
            g[t] = g[t] * inverse
            p[t] = p[t] * inverse

    below = jnp.concatenate(g[8:16], axis=0)[:, 0:64]
    panel(0)
    scaled = jnp.concatenate([jnp.concatenate(g[0:8], axis=0), jnp.concatenate(p[0:8], axis=0)], axis=1)
    update = exact_matmul(below, scaled)
    for t in range(8, 16):
        g[t] = g[t] - update[8 * t - 64:8 * t - 56, 0:NC]
        p[t] = p[t] - update[8 * t - 64:8 * t - 56, NC:]
    panel(8)
    last = jnp.concatenate(p[8:16], axis=0)
    above = turn(scaled[:, 0:NC], 64)[:, 0:64]
    first = scaled[:, NC:] - exact_matmul(above, last)
    weights = jnp.transpose(jnp.concatenate([first, last], axis=0))[0:32]
    high, mid, low = split(weights)
    left_a = jnp.concatenate([jnp.concatenate([high, high], axis=1), jnp.concatenate([mid, mid], axis=1)], axis=0)
    left_b = jnp.concatenate([high, low], axis=1)
    for r in range(0, NR, 2):
        w_high, w_mid, w_low = split(jnp.concatenate([basis[r, 32:160, :], basis[r + 1, 32:160, :]], axis=1))
        moved_a = matmul(left_a, jnp.concatenate([w_high, w_mid], axis=0))
        moved_b = matmul(left_b, jnp.concatenate([w_low, w_high], axis=0))
        moved = moved_a[0:32] + (moved_a[32:64] + moved_b)
        out[pl.ds(r, 32, stride=NR), :] = basis[r, 0:32, :] - moved[:, :NC]
        out[pl.ds(r + 1, 32, stride=NR), :] = basis[r + 1, 0:32, :] - moved[:, NC:]


def far(*dims):
    return jax.ShapeDtypeStruct(dims, F32)


def shape(*dims):
    return far(*dims) if INTERPRET else pltpu.VMEM(dims, F32)


def ring(count, step):
    return [(i, (i + step) % count) for i in range(count)]


def on_device(dom, sub, dom_count, sub_count, reduce_groups, source, initial, lumped_mass, node_slots, stiffness):
    rows_total, cols_total = dom_count * NR, sub_count * NC

    def prepare(*refs):
        prepare_body(dom, sub, rows_total, cols_total, *refs)

    ini_m, src_m, ini_h, src_h, w_main, w_strip, to_left, to_right, to_up, to_down = call(
        prepare,
        (shape(NR, NF, NC), shape(NR, NF, NC), shape(NR, 8, NC), shape(NR, 8, NC), shape(NH, 24, NC), shape(4, 24, NC),
         shape(176, NC), shape(176, NC), shape(MAIN_END, NC), shape(MAIN_END, NC)),
        scratch=[
            pltpu.VMEM((3, NH, 24, NC), F32),
            pltpu.VMEM((NF * NR, NC), F32),
            pltpu.VMEM((NF * NR, NC), F32),
            pltpu.VMEM((NR, NC), F32),
            pltpu.VMEM((6, NR, NC), jnp.int32),
            pltpu.VMEM((36, NR, NC), F32),
            pltpu.SemaphoreType.DMA((5,)),
        ],
        in_specs=[pl.BlockSpec(memory_space=pl.ANY)] * 5,
        name="prepare",
    )(*distant(source.reshape(NF * NR, NC), initial.reshape(NF * NR, NC), lumped_mass, node_slots,
               stiffness.reshape(36, NR, NC)))
    from_right = lax.ppermute(to_left, sub, ring(sub_count, -1))
    from_left = lax.ppermute(to_right, sub, ring(sub_count, 1))
    down_main = lax.ppermute(to_up, dom, ring(dom_count, -1))
    up_main = lax.ppermute(to_down, dom, ring(dom_count, 1))
    def columns(*refs):
        columns_body(sub, sub_count, *refs)

    ini_h, src_h, w_strip, to_up, to_down = call(
        columns,
        (shape(NR, 8, NC), shape(NR, 8, NC), shape(4, 24, NC), shape(STRIP_END, NC), shape(STRIP_END, NC)),
        name="columns",
    )(*near(ini_h, src_h, w_strip, from_left, from_right))
    down_strip = lax.ppermute(to_up, dom, ring(dom_count, -1))
    up_strip = lax.ppermute(to_down, dom, ring(dom_count, 1))

    def products(*refs):
        basis_body(dom, dom_count, 1.0 / float(rows_total * cols_total), *refs)

    basis, packed = call(
        products,
        (shape(NR, 160, NC), shape(40, NC)),
        scratch=[
            pltpu.VMEM((NCOEF, 40, NC), F32),
            pltpu.VMEM((NCOEF, 40, NC), F32),
            pltpu.VMEM((36, 40, NC), F32),
            pltpu.VMEM((36, 40, NC), F32),
            pltpu.VMEM((36, 40, NC), F32),
            pltpu.VMEM((36, 40, NC), F32),
            pltpu.VMEM((96, NC), F32),
        ],
        name="products",
    )(*near(ini_m, src_m, ini_h, src_h, w_main, w_strip, up_main, down_main, up_strip, down_strip))
    for i, (axes, count) in enumerate(reduce_groups):
        if count == 2:
            gathered = jnp.stack([packed, lax.ppermute(packed, axes, [(0, 1), (1, 0)])])
        else:
            gathered = lax.all_to_all(jnp.broadcast_to(packed[None], (count, 40, NC)), axes, 0, 0)
        if i + 1 < len(reduce_groups):
            packed = jnp.sum(gathered, axis=0)
    new_residual, upper = call(
        solve_body,
        (far(NF * NR, NC), far(128, 128)),
        scratch=[pltpu.VMEM((128, NC), F32)],
        name="solve",
    )(*near(gathered, basis))
    return (new_residual.reshape(NF, NR, NC), upper)


def solution(mesh):
    dom_count, sub_count = mesh.shape["dom"], mesh.shape["sub"]
    if dom_count == 64 and sub_count == 4:
        fine = Mesh(mesh.devices.reshape(8, 4, 2, 4), ("z", "x", "c", "sub"))
        dom = ("z", "x", "c")
        groups = ((("c",), 2), (("x", "sub"), 16), (("z",), 8))
    else:
        fine, dom = mesh, ("dom",)
        groups = (("sub", sub_count), ("dom", dom_count))

    def body(*args):
        return on_device(dom, "sub", dom_count, sub_count, groups, *args)

    return jax.shard_map(
        body,
        mesh=fine,
        in_specs=(
            P(None, dom, "sub"),
            P(None, dom, "sub"),
            P(dom, "sub"),
            P(None, dom, "sub"),
            P(None, None, dom, "sub"),
        ),
        out_specs=(P(None, dom, "sub"), P()),
        check_vma=False,
    )
```

```python
import jax
import jax.numpy as jnp
from jax import lax
from jax.experimental import pallas as pl
from jax.experimental.pallas import tpu as pltpu
from jax.sharding import Mesh, PartitionSpec as P


STEPS = 4
NF = 32
NR = 16
NC = 128
INTERPRET = False
F32 = jnp.float32

HALF = [(0, 0), (0, 1), (0, 2)] + [(dr, dc) for dr in (1, 2) for dc in range(-2, 3)]
HALF_INDEX = {d: i for i, d in enumerate(HALF)}
NH = len(HALF)
TURNED = [d for d in HALF if d[1] != 0]
TURNED_INDEX = {d: NH + i for i, d in enumerate(TURNED)}
NCOEF = NH + len(TURNED)


def lanes(shape):
    return lax.broadcasted_iota(jnp.int32, shape, len(shape) - 1)


def turn(value, shift):
    shift = shift % NC
    return value if shift == 0 else pltpu.roll(value, shift, value.ndim - 1)


def call(body, outs, scratch=(), **kw):
    return pl.pallas_call(
        body,
        out_shape=outs,
        scratch_shapes=scratch,
        interpret=INTERPRET,
        compiler_params=pltpu.CompilerParams(vmem_limit_bytes=16 << 20),
        **kw,
    )


def near(*values):
    if INTERPRET:
        return values
    return tuple(pltpu.with_memory_space_constraint(v, pltpu.VMEM) for v in values)


def distant(*values):
    if INTERPRET:
        return values
    return tuple(pltpu.with_memory_space_constraint(v, pltpu.HBM) for v in values)


MAIN_I = 0
MAIN_S = 10 * 32
MAIN_W = MAIN_S + 8 * 32
MAIN_END = MAIN_W + NH * 16
STRIP_I = 0
STRIP_S = 10 * 8
STRIP_W = STRIP_S + 8 * 8
STRIP_END = STRIP_W + 4 * 16


def prepare_body(dom, sub_axis, rows_total, cols_total, source_far, initial_far, mass_far, slots_far, stiffness_far,
                 ini_m, src_m, ini_h, src_h, w_main, w_strip, to_left, to_right, to_up, to_down,
                 acc, source, initial, mass, slots, stiffness, arrived):
    copies = [
        pltpu.make_async_copy(far_ref, near_ref, arrived.at[i])
        for i, (far_ref, near_ref) in enumerate((
            (slots_far, slots), (stiffness_far, stiffness), (mass_far, mass), (initial_far, initial),
            (source_far, source)))
    ]
    for copy in copies:
        copy.start()
    for copy in copies[:3]:
        copy.wait()
    row = lax.broadcasted_iota(jnp.int32, (NR, NC), 0) + lax.axis_index(dom) * NR
    col = lanes((NR, NC)) + lax.axis_index(sub_axis) * NC
    top, bottom = row == 0, row == rows_total - 1
    west, east = col == 0, col == cols_total - 1
    kept = []
    for a in range(6):
        slot = slots[a]
        in_west = (slot == 0) | (slot == 3) | (slot == 6)
        in_east = (slot == 2) | (slot == 5) | (slot == 8)
        outside = (top & (slot < 3)) | (bottom & (slot > 5)) | (west & in_west) | (east & in_east)
        kept.append(jnp.where(outside, 99, slot))
    acc[...] = jnp.zeros(acc.shape, F32)
    zero = jnp.zeros((NR, NC), F32)
    for q in range(9):
        middle = []
        for a in range(6):
            value = zero
            for b in range(6):
                value = jnp.where(kept[b] == q, stiffness[a * 6 + b], value)
            middle.append(value)
        for p in range(q + 1):
            value = zero
            for a in range(6):
                value = jnp.where(kept[a] == p, middle[a], value)
            place = HALF_INDEX[(q // 3 - p // 3, q % 3 - p % 3)]
            start = 7 + p // 3 - 1
            acc[p % 3, place, start:start + NR, :] += value
    acc[1, 0, 7:7 + NR, :] += mass[...]

    lane = lanes((24, NC))
    pack_left = [jnp.zeros((24, NC), F32) for _ in range(2)]
    pack_right = [jnp.zeros((24, NC), F32) for _ in range(2)]
    strips = [jnp.zeros((24, NC), F32) for _ in range(4)]
    for d in range(NH):
        east_turn = turn(acc[2, d], 1)
        west_turn = turn(acc[0, d], -1)
        over_east = jnp.where(lane == 0, east_turn, 0.0)
        over_west = jnp.where(lane == NC - 1, west_turn, 0.0)
        main = acc[1, d] + (east_turn - over_east) + (west_turn - over_west)
        w_main[d] = main
        to_up[MAIN_W + 16 * d:MAIN_W + 16 * d + 16, :] = main[0:16]
        to_down[MAIN_W + 16 * d:MAIN_W + 16 * d + 16, :] = main[8:24]
        own = turn(jnp.where(lane < 4, main, 0.0) + over_west, 28)
        own = own + turn(jnp.where(lane >= 124, main, 0.0) + over_east, 4)
        strips[d // 4] = strips[d // 4] + turn(own, 32 * (d % 4))
        k = 16 * (d % 8)
        pack_right[d // 8] = pack_right[d // 8] + turn(jnp.where(lane >= 118, main, 0.0) + over_east, 12 + k)
        pack_left[d // 8] = pack_left[d // 8] + turn(jnp.where(lane < 10, main, 0.0) + over_west, 4 + k)
    for j in range(4):
        w_strip[j] = strips[j]
    for j in range(2):
        to_right[128 + 24 * j:152 + 24 * j, :] = pack_right[j]
        to_left[128 + 24 * j:152 + 24 * j, :] = pack_left[j]

    for copy in copies[3:]:
        copy.wait()
    lane = lanes((8, NC))
    place = lane % 32
    segment = lane // 32
    for r in range(NR):
        right = jnp.zeros((8, NC), F32)
        left = jnp.zeros((8, NC), F32)
        strip_i = jnp.zeros((8, NC), F32)
        strip_s = jnp.zeros((8, NC), F32)
        for g in range(4):
            here = segment == g
            ini = initial[pl.ds(g * 128 + r, 8, stride=NR), :]
            src = source[pl.ds(g * 128 + r, 8, stride=NR), :]
            at = 8 * g
            ini_m[r, at:at + 8, :] = ini
            src_m[r, at:at + 8, :] = src
            if r < 10:
                to_up[MAIN_I + 32 * r + at:MAIN_I + 32 * r + at + 8, :] = ini
            if r >= 6:
                to_down[MAIN_I + 32 * (r - 6) + at:MAIN_I + 32 * (r - 6) + at + 8, :] = ini
            if r < 8:
                to_up[MAIN_S + 32 * r + at:MAIN_S + 32 * r + at + 8, :] = src
            else:
                to_down[MAIN_S + 32 * (r - 8) + at:MAIN_S + 32 * (r - 8) + at + 8, :] = src
            turned = turn(ini, 4 + 32 * g)
            strip_i = jnp.where(here & (place < 4), turned, strip_i)
            left = jnp.where(here & (place >= 4) & (place < 14), turned, left)
            turned = turn(src, 4 + 32 * g)
            strip_s = jnp.where(here & (place < 4), turned, strip_s)
            left = jnp.where(here & (place >= 20) & (place < 30), turn(src, 20 + 32 * g), left)
            turned = turn(ini, 28 + 32 * g)
            strip_i = jnp.where(here & (place >= 28), turned, strip_i)
            turned = turn(src, 28 + 32 * g)
            strip_s = jnp.where(here & (place >= 28), turned, strip_s)
            right = jnp.where(here & (place >= 18) & (place < 28), turned, right)
            right = jnp.where(here & (place >= 2) & (place < 12), turn(ini, 12 + 32 * g), right)
        ini_h[r] = strip_i
        src_h[r] = strip_s
        to_right[8 * r:8 * r + 8, :] = right
        to_left[8 * r:8 * r + 8, :] = left


def columns_body(sub_axis, sub_count, ini_h, src_h, w_strip, from_left, from_right, ini_o, src_o, strip_o, to_up, to_down):
    lane = lanes((8, NC))
    place = lane % 32
    is_left = (place >= 18) & (place < 28)
    is_right = (place >= 4) & (place < 14)
    at = lax.axis_index(sub_axis)
    has_left, has_right = at > 0, at < sub_count - 1
    for r in range(NR):
        left = jnp.where(has_left, from_left[8 * r:8 * r + 8, :], 0.0)
        right = jnp.where(has_right, from_right[8 * r:8 * r + 8, :], 0.0)
        ini = jnp.where(is_left, turn(left, 16), jnp.where(is_right, right, ini_h[r]))
        src = jnp.where(is_left, left, jnp.where(is_right, turn(right, -16), src_h[r]))
        ini_o[r] = ini
        src_o[r] = src
        if r < 10:
            to_up[STRIP_I + 8 * r:STRIP_I + 8 * r + 8, :] = ini
        if r >= 6:
            to_down[STRIP_I + 8 * (r - 6):STRIP_I + 8 * (r - 6) + 8, :] = ini
        if r < 8:
            to_up[STRIP_S + 8 * r:STRIP_S + 8 * r + 8, :] = src
        else:
            to_down[STRIP_S + 8 * (r - 8):STRIP_S + 8 * (r - 8) + 8, :] = src
    lane = lanes((24, NC))
    strips = [w_strip[j] for j in range(4)]
    for d in range(NH):
        k = 16 * (d % 8)
        left = from_left[128 + 24 * (d // 8):152 + 24 * (d // 8), :]
        right = from_right[128 + 24 * (d // 8):152 + 24 * (d // 8), :]
        left = jnp.where((lane >= 18) & (lane <= 28) & has_left, turn(left, 16 - k), 0.0)
        right = jnp.where((lane >= 3) & (lane <= 13) & has_right, turn(right, -k), 0.0)
        strips[d // 4] = strips[d // 4] + turn(left + right, 32 * (d % 4))
    for j in range(4):
        strip_o[j] = strips[j]
        to_up[STRIP_W + 16 * j:STRIP_W + 16 * j + 16, :] = strips[j][0:16]
        to_down[STRIP_W + 16 * j:STRIP_W + 16 * j + 16, :] = strips[j][8:24]


def basis_body(dom, dom_count, scale, ini_m, src_m, ini_h, src_h, w_main, w_strip, up_main, down_main, up_strip, down_strip,
               basis, packed,
               coef_m, coef_h, ini_v, src_v, vec_a, vec_b, sums):
    lane = lanes((8, NC))
    segment = lane // 32
    own = (1, 2, 3)
    at = lax.axis_index(dom)
    has_up, has_down = at > 0, at < dom_count - 1

    def upper(ref, start, size=8):
        return jnp.where(has_up, ref[start:start + size, :], 0.0)

    def lower(ref, start, size=8):
        return jnp.where(has_down, ref[start:start + size, :], 0.0)

    for d in range(NH):
        for t in range(5):
            main = None
            strip = None
            parts = []
            if t < 2:
                parts.append((upper(up_main, MAIN_W + 16 * d + 8 * t), upper(up_strip, STRIP_W + 16 * (d // 4) + 8 * t)))
            if t in own:
                parts.append((w_main[d, 8 * t - 8:8 * t, :], w_strip[d // 4, 8 * t - 8:8 * t, :]))
            if t > 2:
                s = 8 * (t - 3)
                parts.append((lower(down_main, MAIN_W + 16 * d + s), lower(down_strip, STRIP_W + 16 * (d // 4) + s)))
            main = sum(p[0] for p in parts[1:]) + parts[0][0] if len(parts) > 1 else parts[0][0]
            strip = sum(p[1] for p in parts[1:]) + parts[0][1] if len(parts) > 1 else parts[0][1]
            strip = jnp.where(segment == d % 4, strip, 0.0)
            strip = strip + turn(strip, 32)
            strip = strip + turn(strip, 64)
            main = jnp.where(lane == 0, turn(strip, -28), main)
            main = jnp.where(lane == NC - 1, turn(strip, 124), main)
            coef_m[d, 8 * t:8 * t + 8, :] = main
            coef_h[d, 8 * t:8 * t + 8, :] = strip
            dc = HALF[d][1]
            if dc != 0:
                turned = turn(main, dc)
                if dc > 0:
                    turned = jnp.where(lane < dc, turn(strip, dc - 28), turned)
                else:
                    turned = jnp.where(lane >= NC + dc, turn(strip, dc + 124), turned)
                i = TURNED_INDEX[HALF[d]]
                coef_m[i, 8 * t:8 * t + 8, :] = turned
                coef_h[i, 8 * t:8 * t + 8, :] = turn(strip, dc)

    for i in range(10):
        ini_v[i, 0:32] = upper(up_main, MAIN_I + 32 * i, 32)
        ini_v[i, 32:40] = upper(up_strip, STRIP_I + 8 * i)
        ini_v[26 + i, 0:32] = lower(down_main, MAIN_I + 32 * i, 32)
        ini_v[26 + i, 32:40] = lower(down_strip, STRIP_I + 8 * i)
    for i in range(8):
        src_v[2 + i, 0:32] = upper(up_main, MAIN_S + 32 * i, 32)
        src_v[2 + i, 32:40] = upper(up_strip, STRIP_S + 8 * i)
        src_v[26 + i, 0:32] = lower(down_main, MAIN_S + 32 * i, 32)
        src_v[26 + i, 32:40] = lower(down_strip, STRIP_S + 8 * i)
    for i in range(NR):
        ini_v[10 + i, 0:32] = ini_m[i]
        ini_v[10 + i, 32:40] = ini_h[i]
        src_v[10 + i, 0:32] = src_m[i]
        src_v[10 + i, 32:40] = src_h[i]

    place = lane % 32
    edge = (lane < 2) | (lane >= NC - 2)
    from_low = place < 2
    tail = place >= 30
    second = (lane >= 16) & (lane < 48)
    upper_pair = (lane >= 48) & (lane < 112)

    def edges_of(strip):
        both = jnp.where(from_low, turn(strip, -28), turn(strip, -4))
        return [turn(both, -32 * g) for g in range(4)]

    def inner_of(mains, strip):
        low = jnp.where(second, turn(mains[1], 32), mains[0])
        high = jnp.where(second, turn(mains[3], 32), mains[2])
        both = jnp.where(upper_pair, turn(high, 64), low)
        return jnp.where(tail, turn(both, 28), jnp.where(from_low, turn(both, 4), strip))

    def image(vec, r):
        def spread(ref):
            coef = {}
            for dr in range(-2, 3):
                for dc in range(-2, 3):
                    if (dr, dc) in HALF_INDEX:
                        index = TURNED_INDEX[(dr, dc)] if dc != 0 else HALF_INDEX[(dr, dc)]
                        at = r + 15
                    else:
                        index = HALF_INDEX[(-dr, -dc)]
                        at = r + 15 + dr
                    coef[(dr, dc)] = jnp.broadcast_to(ref[index, pl.ds(at, 1), :], (8, NC))
            return coef

        def unit(coef, u):
            near = [vec[r + 10 + dr, 8 * u:8 * u + 8, :] for dr in range(-2, 3)]
            parts = []
            for dc in (-2, 2, -1, 1, 0):
                part = None
                for dr in range(-2, 3):
                    term = coef[(dr, dc)] * near[dr + 2]
                    part = term if part is None else part + term
                parts.append(turn(part, -dc))
            return ((parts[0] + parts[1]) + (parts[2] + parts[3])) + parts[4]

        strip = unit(spread(coef_h), 4)
        coef = spread(coef_m)
        edges = edges_of(strip)
        result = [jnp.where(edge, edges[g], unit(coef, g)) for g in range(4)]
        return result + [strip]

    def mended(vec, r):
        mains = [vec[r + 10, 8 * g:8 * g + 8, :] for g in range(4)]
        return inner_of(mains, vec[r + 10, 32:40, :])

    def mend(vec, rows):
        strips = [mended(vec, r) for r in rows]
        for r, strip in zip(rows, strips):
            vec[r + 10, 32:40, :] = strip

    vectors = (vec_a, vec_b)
    for step in range(-1, STEPS):
        reach = 6 - 2 * step
        source_vec = ini_v if step < 0 else vectors[step % 2]
        target_vec = vec_a if step < 0 else vectors[(step + 1) % 2]

        def some_rows(rows, before, inside, step=step, source_vec=source_vec, target_vec=target_vec):
            more = step + 1 < STEPS
            strips = [mended(target_vec, r) for r in before] if more else []
            values = []
            for r in rows:
                units = image(source_vec, r)
                olds = src_v if step < 0 else source_vec
                nexts = []
                if more:
                    for u in range(5):
                        old = olds[r + 10, 8 * u:8 * u + 8, :]
                        nexts.append(old - units[u] if step < 0 else units[u] - 2.0 * old)
                values.append((r, units, nexts))
            for r, strip in zip(before, strips):
                target_vec[r + 10, 32:40, :] = strip
            for r, units, nexts in values:
                for u, value in enumerate(nexts):
                    target_vec[r + 10, 8 * u:8 * u + 8, :] = value
                if inside:
                    kept = nexts if step < 0 else units
                    for u in range(4):
                        at = 32 + 32 * step + 8 * u
                        basis[r, at:at + 8, :] = kept[u]

        def outer_rows(i, reach=reach):
            return (2 * i - reach, 2 * i - reach + 1, NR + 2 * i, NR + 2 * i + 1)

        def middle_rows(i):
            return tuple(4 * i + j for j in range(4))

        def outer(i, carry, some_rows=some_rows, outer_rows=outer_rows):
            some_rows(outer_rows(i), outer_rows(jnp.maximum(i - 1, 0)), False)
            return carry

        def middle(i, carry, some_rows=some_rows):
            some_rows(middle_rows(i), middle_rows(jnp.maximum(i - 1, 0)), True)
            return carry

        last = middle_rows(NR // 4 - 1)
        if reach > 0:
            lax.fori_loop(0, reach // 2, outer, 0)
            last = last + outer_rows(reach // 2 - 1)
        lax.fori_loop(0, NR // 4, middle, 0)
        if step + 1 < STEPS:
            mend(target_vec, last)

    sums[...] = jnp.zeros(sums.shape, F32)

    def product(i, carry):
        total = None
        for j in range(2):
            r = 4 * i + 2 * j
            high, mid, low = split(jnp.concatenate([basis[r], basis[r + 1]], axis=1))
            left = [jnp.concatenate([x[0:32], x[96:160]], axis=0) for x in (high, mid, low)]
            both = jnp.concatenate([high[32:], mid[32:]], axis=0)
            hh = matmul_t(left[0], both)
            mm = matmul_t(left[1], both)
            rest = matmul_t(left[2], high[32:]) + matmul_t(left[0], low[32:])
            part = ((rest + mm[:, NC:]) + (hh[:, NC:] + mm[:, :NC])) + hh[:, :NC]
            total = part if total is None else total + part
        sums[...] += total
        return carry

    lax.fori_loop(0, NR // 4, product, 0)
    lane = lanes((32, NC))
    low_half = sums[0:32, :] * scale
    high_half = jnp.where(lane < 64, turn(sums[32:64, :], -32), sums[64:96, :]) * scale
    row = lax.broadcasted_iota(jnp.int32, (32, NC), 0)
    within = lane % 32
    packed[0:32, :] = jnp.where(within >= row, low_half, high_half)
    diagonal = jnp.sum(jnp.where(within == row, high_half, 0.0), axis=0, keepdims=True)
    packed[32:40, :] = jnp.broadcast_to(diagonal, (8, NC))


def split(value):
    high = value.astype(jnp.bfloat16)
    value = value - high.astype(F32)
    mid = value.astype(jnp.bfloat16)
    return high, mid, (value - mid.astype(F32)).astype(jnp.bfloat16)


def matmul_t(a, b):
    return lax.dot_general(a, b, (((1,), (1,)), ((), ())), preferred_element_type=F32)


def matmul(a, b):
    return lax.dot_general(a, b, (((1,), (0,)), ((), ())), preferred_element_type=F32)


def exact_matmul(a, b):
    return lax.dot_general(a, b, (((1,), (0,)), ((), ())), precision=lax.Precision.HIGHEST,
                           preferred_element_type=F32)


def solve_body(parts, basis, out, upper, raw):
    total = parts[0]
    for i in range(1, parts.shape[0]):
        total = total + parts[i]
    half = total[0:32]
    lane = lanes((32, NC))
    row = lax.broadcasted_iota(jnp.int32, (32, NC), 0)
    within = lane % 32
    block = lane // 32
    flipped = jnp.transpose(jnp.concatenate([half] * 4, axis=0))
    mirror = flipped[0:32]
    for b in range(1, 4):
        mirror = jnp.where(block == b, flipped[32 * b:32 * b + 32], mirror)
    project = jnp.where(within >= row, half, mirror)
    later = jnp.where(within < row, half, jnp.where(within > row, mirror, jnp.broadcast_to(total[32:33], (32, NC))))
    early = project + 2.0 * turn(project, 32)
    gram = [
        jnp.where(block == 3, turn(later, -32), turn(early, -32)),
        jnp.where(block < 2, turn(early, 64), turn(later, 64)),
        jnp.where(block < 1, turn(early, 32), turn(later, 32)),
        later,
    ]
    right = [jnp.where(lane < 32, turn(project, -32 * b), 0.0) for b in range(4)]
    g = [gram[t // 4][8 * (t % 4):8 * (t % 4) + 8] for t in range(16)]
    p = [right[t // 4][8 * (t % 4):8 * (t % 4) + 8] for t in range(16)]
    lane = lanes((8, NC))
    sub = lax.broadcasted_iota(jnp.int32, (8, NC), 0)

    def spread(value, j):
        return jnp.broadcast_to(value[j:j + 1, :], (8, NC))

    def columns(value, base):
        return [jnp.broadcast_to(value[:, base + q:base + q + 1], (8, NC)) for q in range(8)]

    def panel(first):
        for t in range(first, first + 8):
            col = columns(g[t], 8 * t)
            steps = []
            for j in range(8):
                inverse = 1.0 / spread(col[j], j)
                raw[8 * t + j:8 * t + j + 1, :] = g[t][j:j + 1, :]
                u = spread(g[t], j) * inverse
                up = spread(p[t], j) * inverse
                m = jnp.where(sub == j, 0.0, col[j])
                scaled_cols = {}
                for q in range(j + 1, 8):
                    scaled_cols[q] = spread(col[q], j) * inverse
                    col[q] = col[q] - m * scaled_cols[q]
                g[t] = g[t] - m * u
                p[t] = p[t] - m * up
                steps.append((scaled_cols, u, up))
            for i in [first + (t - first + n) % 8 for n in range(1, 8)]:
                col = columns(g[i], 8 * t)
                for j in range(8):
                    scaled_cols, u, up = steps[j]
                    for q in range(j + 1, 8):
                        col[q] = col[q] - col[j] * scaled_cols[q]
                    g[i] = g[i] - col[j] * u
                    p[i] = p[i] - col[j] * up
        for t in range(first, first + 8):
            line = raw[8 * t:8 * t + 8, :]
            diagonal = jnp.sum(jnp.where(lane == sub + 8 * t, line, 0.0), axis=1, keepdims=True)
            diagonal = jnp.broadcast_to(diagonal, (8, NC))
            upper[8 * t:8 * t + 8, :] = jnp.where(lane >= sub + 8 * t, line / jnp.sqrt(diagonal), 0.0)
            inverse = 1.0 / diagonal
            g[t] = g[t] * inverse
            p[t] = p[t] * inverse

    below = jnp.concatenate(g[8:16], axis=0)[:, 0:64]
    panel(0)
    scaled = jnp.concatenate([jnp.concatenate(g[0:8], axis=0), jnp.concatenate(p[0:8], axis=0)], axis=1)
    update = exact_matmul(below, scaled)
    for t in range(8, 16):
        g[t] = g[t] - update[8 * t - 64:8 * t - 56, 0:NC]
        p[t] = p[t] - update[8 * t - 64:8 * t - 56, NC:]
    panel(8)
    last = jnp.concatenate(p[8:16], axis=0)
    above = turn(scaled[:, 0:NC], 64)[:, 0:64]
    first = scaled[:, NC:] - exact_matmul(above, last)
    weights = jnp.transpose(jnp.concatenate([first, last], axis=0))[0:32]
    high, mid, low = split(weights)
    left_a = jnp.concatenate([jnp.concatenate([high, high], axis=1), jnp.concatenate([mid, mid], axis=1)], axis=0)
    left_b = jnp.concatenate([high, low], axis=1)
    for r in range(0, NR, 2):
        w_high, w_mid, w_low = split(jnp.concatenate([basis[r, 32:160, :], basis[r + 1, 32:160, :]], axis=1))
        moved_a = matmul(left_a, jnp.concatenate([w_high, w_mid], axis=0))
        moved_b = matmul(left_b, jnp.concatenate([w_low, w_high], axis=0))
        moved = moved_a[0:32] + (moved_a[32:64] + moved_b)
        out[pl.ds(r, 32, stride=NR), :] = basis[r, 0:32, :] - moved[:, :NC]
        out[pl.ds(r + 1, 32, stride=NR), :] = basis[r + 1, 0:32, :] - moved[:, NC:]


def far(*dims):
    return jax.ShapeDtypeStruct(dims, F32)


def shape(*dims):
    return far(*dims) if INTERPRET else pltpu.VMEM(dims, F32)


def ring(count, step):
    return [(i, (i + step) % count) for i in range(count)]


def on_device(dom, sub, dom_count, sub_count, reduce_groups, source, initial, lumped_mass, node_slots, stiffness):
    rows_total, cols_total = dom_count * NR, sub_count * NC

    def prepare(*refs):
        prepare_body(dom, sub, rows_total, cols_total, *refs)

    ini_m, src_m, ini_h, src_h, w_main, w_strip, to_left, to_right, to_up, to_down = call(
        prepare,
        (shape(NR, NF, NC), shape(NR, NF, NC), shape(NR, 8, NC), shape(NR, 8, NC), shape(NH, 24, NC), shape(4, 24, NC),
         shape(176, NC), shape(176, NC), shape(MAIN_END, NC), shape(MAIN_END, NC)),
        scratch=[
            pltpu.VMEM((3, NH, 24, NC), F32),
            pltpu.VMEM((NF * NR, NC), F32),
            pltpu.VMEM((NF * NR, NC), F32),
            pltpu.VMEM((NR, NC), F32),
            pltpu.VMEM((6, NR, NC), jnp.int32),
            pltpu.VMEM((36, NR, NC), F32),
            pltpu.SemaphoreType.DMA((5,)),
        ],
        in_specs=[pl.BlockSpec(memory_space=pl.ANY)] * 5,
        name="prepare",
    )(*distant(source.reshape(NF * NR, NC), initial.reshape(NF * NR, NC), lumped_mass, node_slots,
               stiffness.reshape(36, NR, NC)))
    from_right = lax.ppermute(to_left, sub, ring(sub_count, -1))
    from_left = lax.ppermute(to_right, sub, ring(sub_count, 1))
    down_main = lax.ppermute(to_up, dom, ring(dom_count, -1))
    up_main = lax.ppermute(to_down, dom, ring(dom_count, 1))

    def columns(*refs):
        columns_body(sub, sub_count, *refs)

    ini_h, src_h, w_strip, to_up, to_down = call(
        columns,
        (shape(NR, 8, NC), shape(NR, 8, NC), shape(4, 24, NC), shape(STRIP_END, NC), shape(STRIP_END, NC)),
        name="columns",
    )(*near(ini_h, src_h, w_strip, from_left, from_right))
    down_strip = lax.ppermute(to_up, dom, ring(dom_count, -1))
    up_strip = lax.ppermute(to_down, dom, ring(dom_count, 1))

    def products(*refs):
        basis_body(dom, dom_count, 1.0 / float(rows_total * cols_total), *refs)

    basis, packed = call(
        products,
        (shape(NR, 160, NC), shape(40, NC)),
        scratch=[
            pltpu.VMEM((NCOEF, 40, NC), F32),
            pltpu.VMEM((NCOEF, 40, NC), F32),
            pltpu.VMEM((36, 40, NC), F32),
            pltpu.VMEM((36, 40, NC), F32),
            pltpu.VMEM((36, 40, NC), F32),
            pltpu.VMEM((36, 40, NC), F32),
            pltpu.VMEM((96, NC), F32),
        ],
        name="products",
    )(*near(ini_m, src_m, ini_h, src_h, w_main, w_strip, up_main, down_main, up_strip, down_strip))
    for i, (axes, count) in enumerate(reduce_groups):
        if count == 2:
            gathered = jnp.stack([packed, lax.ppermute(packed, axes, [(0, 1), (1, 0)])])
        else:
            gathered = lax.all_to_all(jnp.broadcast_to(packed[None], (count, 40, NC)), axes, 0, 0)
        if i + 1 < len(reduce_groups):
            packed = jnp.sum(gathered, axis=0)
    new_residual, upper = call(
        solve_body,
        (far(NF * NR, NC), far(128, 128)),
        scratch=[pltpu.VMEM((128, NC), F32)],
        name="solve",
    )(*near(gathered, basis))
    return (new_residual.reshape(NF, NR, NC), upper)


def solution(mesh):
    dom_count, sub_count = mesh.shape["dom"], mesh.shape["sub"]
    if dom_count == 64 and sub_count == 4:
        fine = Mesh(mesh.devices.reshape(8, 4, 2, 4), ("z", "x", "c", "sub"))
        dom = ("z", "x", "c")
        groups = ((("c",), 2), (("x", "sub"), 16), (("z",), 8))
    else:
        fine, dom = mesh, ("dom",)
        groups = (("sub", sub_count), ("dom", dom_count))

    def body(*args):
        return on_device(dom, "sub", dom_count, sub_count, groups, *args)

    return jax.shard_map(
        body,
        mesh=fine,
        in_specs=(
            P(None, dom, "sub"),
            P(None, dom, "sub"),
            P(dom, "sub"),
            P(None, dom, "sub"),
            P(None, None, dom, "sub"),
        ),
        out_specs=(P(None, dom, "sub"), P()),
        check_vma=False,
    )
```

```python
import jax
import jax.numpy as jnp
from jax import lax
from jax.experimental import pallas as pl
from jax.experimental.pallas import tpu as pltpu
from jax.sharding import Mesh, PartitionSpec as P


STEPS = 4
NF = 32
NR = 16
NC = 128
INTERPRET = False
F32 = jnp.float32

HALF = [(0, 0), (0, 1), (0, 2)] + [(dr, dc) for dr in (1, 2) for dc in range(-2, 3)]
HALF_INDEX = {d: i for i, d in enumerate(HALF)}
NH = len(HALF)
TURNED = [d for d in HALF if d[1] != 0]
TURNED_INDEX = {d: NH + i for i, d in enumerate(TURNED)}
NCOEF = NH + len(TURNED)


def lanes(shape):
    return lax.broadcasted_iota(jnp.int32, shape, len(shape) - 1)


def turn(value, shift):
    shift = shift % NC
    return value if shift == 0 else pltpu.roll(value, shift, value.ndim - 1)


def call(body, outs, scratch=(), **kw):
    return pl.pallas_call(
        body,
        out_shape=outs,
        scratch_shapes=scratch,
        interpret=INTERPRET,
        compiler_params=pltpu.CompilerParams(vmem_limit_bytes=16 << 20),
        **kw,
    )


def near(*values):
    if INTERPRET:
        return values
    return tuple(pltpu.with_memory_space_constraint(v, pltpu.VMEM) for v in values)


def distant(*values):
    if INTERPRET:
        return values
    return tuple(pltpu.with_memory_space_constraint(v, pltpu.HBM) for v in values)


MAIN_I = 0
MAIN_S = 10 * 32
MAIN_W = MAIN_S + 8 * 32
MAIN_END = MAIN_W + NH * 16
STRIP_I = 0
STRIP_S = 10 * 8
STRIP_W = STRIP_S + 8 * 8
STRIP_END = STRIP_W + 4 * 16


def prepare_body(dom, sub_axis, rows_total, cols_total, source_far, initial_far, mass_far, slots_far, stiffness_far,
                 ini_m, src_m, ini_h, src_h, w_main, w_strip, to_left, to_right, to_up, to_down,
                 acc, source, initial, mass, slots, stiffness, arrived):
    copies = [
        pltpu.make_async_copy(far_ref, near_ref, arrived.at[i])
        for i, (far_ref, near_ref) in enumerate((
            (slots_far, slots), (stiffness_far, stiffness), (mass_far, mass), (initial_far, initial),
            (source_far, source)))
    ]
    for copy in copies:
        copy.start()
    for copy in copies[:3]:
        copy.wait()
    row = lax.broadcasted_iota(jnp.int32, (NR, NC), 0) + lax.axis_index(dom) * NR
    col = lanes((NR, NC)) + lax.axis_index(sub_axis) * NC
    top, bottom = row == 0, row == rows_total - 1
    west, east = col == 0, col == cols_total - 1
    kept = []
    for a in range(6):
        slot = slots[a]
        in_west = (slot == 0) | (slot == 3) | (slot == 6)
        in_east = (slot == 2) | (slot == 5) | (slot == 8)
        outside = (top & (slot < 3)) | (bottom & (slot > 5)) | (west & in_west) | (east & in_east)
        kept.append(jnp.where(outside, 99, slot))
    acc[...] = jnp.zeros(acc.shape, F32)
    zero = jnp.zeros((NR, NC), F32)
    for q in range(9):
        middle = []
        for a in range(6):
            value = zero
            for b in range(6):
                value = jnp.where(kept[b] == q, stiffness[a * 6 + b], value)
            middle.append(value)
        for p in range(q + 1):
            value = zero
            for a in range(6):
                value = jnp.where(kept[a] == p, middle[a], value)
            place = HALF_INDEX[(q // 3 - p // 3, q % 3 - p % 3)]
            start = 7 + p // 3 - 1
            acc[p % 3, place, start:start + NR, :] += value
    acc[1, 0, 7:7 + NR, :] += mass[...]

    lane = lanes((24, NC))
    pack_left = [jnp.zeros((24, NC), F32) for _ in range(2)]
    pack_right = [jnp.zeros((24, NC), F32) for _ in range(2)]
    strips = [jnp.zeros((24, NC), F32) for _ in range(4)]
    for d in range(NH):
        east_turn = turn(acc[2, d], 1)
        west_turn = turn(acc[0, d], -1)
        over_east = jnp.where(lane == 0, east_turn, 0.0)
        over_west = jnp.where(lane == NC - 1, west_turn, 0.0)
        main = acc[1, d] + (east_turn - over_east) + (west_turn - over_west)
        w_main[d] = main
        to_up[MAIN_W + 16 * d:MAIN_W + 16 * d + 16, :] = main[0:16]
        to_down[MAIN_W + 16 * d:MAIN_W + 16 * d + 16, :] = main[8:24]
        own = turn(jnp.where(lane < 4, main, 0.0) + over_west, 28)
        own = own + turn(jnp.where(lane >= 124, main, 0.0) + over_east, 4)
        strips[d // 4] = strips[d // 4] + turn(own, 32 * (d % 4))
        k = 16 * (d % 8)
        pack_right[d // 8] = pack_right[d // 8] + turn(jnp.where(lane >= 118, main, 0.0) + over_east, 12 + k)
        pack_left[d // 8] = pack_left[d // 8] + turn(jnp.where(lane < 10, main, 0.0) + over_west, 4 + k)
    for j in range(4):
        w_strip[j] = strips[j]
    for j in range(2):
        to_right[128 + 24 * j:152 + 24 * j, :] = pack_right[j]
        to_left[128 + 24 * j:152 + 24 * j, :] = pack_left[j]

    for copy in copies[3:]:
        copy.wait()
    lane = lanes((8, NC))
    place = lane % 32
    second = (lane >= 16) & (lane < 48)
    upper_pair = (lane >= 48) & (lane < 112)

    def edges(tiles):
        low = jnp.where(second, turn(tiles[1], 32), tiles[0])
        high = jnp.where(second, turn(tiles[3], 32), tiles[2])
        return jnp.where(upper_pair, turn(high, 64), low)

    zero = jnp.zeros((8, NC), F32)
    for r in range(NR):
        inis = [initial[pl.ds(g * 128 + r, 8, stride=NR), :] for g in range(4)]
        srcs = [source[pl.ds(g * 128 + r, 8, stride=NR), :] for g in range(4)]
        for g in range(4):
            at, ini, src = 8 * g, inis[g], srcs[g]
            ini_m[r, at:at + 8, :] = ini
            src_m[r, at:at + 8, :] = src
            if r < 10:
                to_up[MAIN_I + 32 * r + at:MAIN_I + 32 * r + at + 8, :] = ini
            if r >= 6:
                to_down[MAIN_I + 32 * (r - 6) + at:MAIN_I + 32 * (r - 6) + at + 8, :] = ini
            if r < 8:
                to_up[MAIN_S + 32 * r + at:MAIN_S + 32 * r + at + 8, :] = src
            else:
                to_down[MAIN_S + 32 * (r - 8) + at:MAIN_S + 32 * (r - 8) + at + 8, :] = src
        ini, src = edges(inis), edges(srcs)
        ini_east, ini_west, src_east, src_west = turn(ini, 4), turn(ini, 28), turn(src, 4), turn(src, 28)
        strip_i = jnp.where(place < 4, ini_east, jnp.where(place >= 28, ini_west, zero))
        strip_s = jnp.where(place < 4, src_east, jnp.where(place >= 28, src_west, zero))
        left = jnp.where((place >= 4) & (place < 14), ini_east, turn(src, 20))
        left = jnp.where((place >= 4) & (place < 30), left, zero)
        right = jnp.where((place >= 18) & (place < 28), src_west, turn(ini, 12))
        right = jnp.where((place >= 2) & (place < 28), right, zero)
        ini_h[r] = strip_i
        src_h[r] = strip_s
        to_right[8 * r:8 * r + 8, :] = right
        to_left[8 * r:8 * r + 8, :] = left


def columns_body(sub_axis, sub_count, ini_h, src_h, w_strip, from_left, from_right, ini_o, src_o, strip_o, to_up, to_down):
    lane = lanes((8, NC))
    place = lane % 32
    is_left = (place >= 18) & (place < 28)
    is_right = (place >= 4) & (place < 14)
    at = lax.axis_index(sub_axis)
    has_left, has_right = at > 0, at < sub_count - 1
    for r in range(NR):
        left = jnp.where(has_left, from_left[8 * r:8 * r + 8, :], 0.0)
        right = jnp.where(has_right, from_right[8 * r:8 * r + 8, :], 0.0)
        ini = jnp.where(is_left, turn(left, 16), jnp.where(is_right, right, ini_h[r]))
        src = jnp.where(is_left, left, jnp.where(is_right, turn(right, -16), src_h[r]))
        ini_o[r] = ini
        src_o[r] = src
        if r < 10:
            to_up[STRIP_I + 8 * r:STRIP_I + 8 * r + 8, :] = ini
        if r >= 6:
            to_down[STRIP_I + 8 * (r - 6):STRIP_I + 8 * (r - 6) + 8, :] = ini
        if r < 8:
            to_up[STRIP_S + 8 * r:STRIP_S + 8 * r + 8, :] = src
        else:
            to_down[STRIP_S + 8 * (r - 8):STRIP_S + 8 * (r - 8) + 8, :] = src
    lane = lanes((24, NC))
    strips = [w_strip[j] for j in range(4)]
    for d in range(NH):
        k = 16 * (d % 8)
        left = from_left[128 + 24 * (d // 8):152 + 24 * (d // 8), :]
        right = from_right[128 + 24 * (d // 8):152 + 24 * (d // 8), :]
        left = jnp.where((lane >= 18) & (lane <= 28) & has_left, turn(left, 16 - k), 0.0)
        right = jnp.where((lane >= 3) & (lane <= 13) & has_right, turn(right, -k), 0.0)
        strips[d // 4] = strips[d // 4] + turn(left + right, 32 * (d % 4))
    for j in range(4):
        strip_o[j] = strips[j]
        to_up[STRIP_W + 16 * j:STRIP_W + 16 * j + 16, :] = strips[j][0:16]
        to_down[STRIP_W + 16 * j:STRIP_W + 16 * j + 16, :] = strips[j][8:24]


def basis_body(dom, dom_count, scale, ini_m, src_m, ini_h, src_h, w_main, w_strip, up_main, down_main, up_strip, down_strip,
               basis, packed,
               coef_m, coef_h, ini_v, vec_a, vec_b, sums):
    lane = lanes((8, NC))
    segment = lane // 32
    own = (1, 2, 3)
    at = lax.axis_index(dom)
    has_up, has_down = at > 0, at < dom_count - 1

    def upper(ref, start, size=8):
        return jnp.where(has_up, ref[pl.ds(start, size), :], 0.0)

    def lower(ref, start, size=8):
        return jnp.where(has_down, ref[pl.ds(start, size), :], 0.0)

    for t in range(5):
        for d in range(NH):
            main = None
            strip = None
            parts = []
            if t < 2:
                parts.append((upper(up_main, MAIN_W + 16 * d + 8 * t), upper(up_strip, STRIP_W + 16 * (d // 4) + 8 * t)))
            if t in own:
                parts.append((w_main[d, 8 * t - 8:8 * t, :], w_strip[d // 4, 8 * t - 8:8 * t, :]))
            if t > 2:
                s = 8 * (t - 3)
                parts.append((lower(down_main, MAIN_W + 16 * d + s), lower(down_strip, STRIP_W + 16 * (d // 4) + s)))
            main = sum(p[0] for p in parts[1:]) + parts[0][0] if len(parts) > 1 else parts[0][0]
            strip = sum(p[1] for p in parts[1:]) + parts[0][1] if len(parts) > 1 else parts[0][1]
            if d % 4 == 0:
                packed_strip = [turn(strip, 32 * n) for n in range(4)]
            strip = packed_strip[(3 - d) % 4]
            for n in range(3):
                strip = jnp.where(segment == n, packed_strip[(n - d) % 4], strip)
            west, east = turn(strip, -28), turn(strip, -4)
            main = jnp.where(lane == 0, west, jnp.where(lane == NC - 1, east, main))
            coef_m[d, 8 * t:8 * t + 8, :] = main
            coef_h[d, 8 * t:8 * t + 8, :] = strip
            dc = HALF[d][1]
            if dc != 0:
                beyond = jnp.where(lane >= 126, west, main) if dc > 0 else jnp.where(lane < 2, east, main)
                i = TURNED_INDEX[HALF[d]]
                coef_m[i, 8 * t:8 * t + 8, :] = turn(beyond, dc)
                coef_h[i, 8 * t:8 * t + 8, :] = turn(strip, dc)

    for i in range(10):
        ini_v[i, 0:32] = upper(up_main, MAIN_I + 32 * i, 32)
        ini_v[i, 32:40] = upper(up_strip, STRIP_I + 8 * i)
        ini_v[26 + i, 0:32] = lower(down_main, MAIN_I + 32 * i, 32)
        ini_v[26 + i, 32:40] = lower(down_strip, STRIP_I + 8 * i)
    for i in range(NR):
        ini_v[10 + i, 0:32] = ini_m[i]
        ini_v[10 + i, 32:40] = ini_h[i]

    def source_tile(r, u, side):
        if side == 0:
            return src_m[r, 8 * u:8 * u + 8, :] if u < 4 else src_h[r]
        i = r + 8 if side < 0 else r - NR
        pick, main, strip = (upper, up_main, up_strip) if side < 0 else (lower, down_main, down_strip)
        if u < 4:
            return pick(main, pl.multiple_of(MAIN_S + 32 * i + 8 * u, 8))
        return pick(strip, pl.multiple_of(STRIP_S + 8 * i, 8))


    place = lane % 32
    edge = (lane < 2) | (lane >= NC - 2)
    from_low = place < 2
    tail = place >= 30
    second = (lane >= 16) & (lane < 48)
    upper_pair = (lane >= 48) & (lane < 112)

    def edges_of(strip):
        both = jnp.where(from_low, turn(strip, -28), turn(strip, -4))
        return [turn(both, -32 * g) for g in range(4)]

    def inner_of(mains, strip):
        low = jnp.where(second, turn(mains[1], 32), mains[0])
        high = jnp.where(second, turn(mains[3], 32), mains[2])
        both = jnp.where(upper_pair, turn(high, 64), low)
        return jnp.where(tail, turn(both, 28), jnp.where(from_low, turn(both, 4), strip))

    def image(vec, r):
        def spread(ref):
            coef = {}
            for dr in range(-2, 3):
                for dc in range(-2, 3):
                    if (dr, dc) in HALF_INDEX:
                        index = TURNED_INDEX[(dr, dc)] if dc != 0 else HALF_INDEX[(dr, dc)]
                        at = r + 15
                    else:
                        index = HALF_INDEX[(-dr, -dc)]
                        at = r + 15 + dr
                    coef[(dr, dc)] = jnp.broadcast_to(ref[index, pl.ds(at, 1), :], (8, NC))
            return coef

        def unit(coef, u):
            near = [vec[r + 10 + dr, 8 * u:8 * u + 8, :] for dr in range(-2, 3)]
            parts = []
            for dc in (-2, 2, -1, 1, 0):
                part = None
                for dr in range(-2, 3):
                    term = coef[(dr, dc)] * near[dr + 2]
                    part = term if part is None else part + term
                parts.append(turn(part, -dc))
            return ((parts[0] + parts[1]) + (parts[2] + parts[3])) + parts[4]

        strip = unit(spread(coef_h), 4)
        coef = spread(coef_m)
        edges = edges_of(strip)
        result = [jnp.where(edge, edges[g], unit(coef, g)) for g in range(4)]
        return result + [strip]

    def mended(vec, r):
        mains = [vec[r + 10, 8 * g:8 * g + 8, :] for g in range(4)]
        return inner_of(mains, vec[r + 10, 32:40, :])

    def mend(vec, rows):
        strips = [mended(vec, r) for r in rows]
        for r, strip in zip(rows, strips):
            vec[r + 10, 32:40, :] = strip

    vectors = (vec_a, vec_b)
    for step in range(-1, STEPS):
        reach = 6 - 2 * step
        source_vec = ini_v if step < 0 else vectors[step % 2]
        target_vec = vec_a if step < 0 else vectors[(step + 1) % 2]

        def some_rows(rows, before, inside, step=step, source_vec=source_vec, target_vec=target_vec):
            more = step + 1 < STEPS
            strips = [mended(target_vec, r) for r in before] if more else []
            values = []
            for n, r in enumerate(rows):
                units = image(source_vec, r)
                side = 0 if inside else (-1 if n < 2 else 1)
                nexts = []
                if more:
                    for u in range(5):
                        old = source_tile(r, u, side) if step < 0 else source_vec[r + 10, 8 * u:8 * u + 8, :]
                        nexts.append(old - units[u] if step < 0 else units[u] - 2.0 * old)
                values.append((r, units, nexts))
            for r, strip in zip(before, strips):
                target_vec[r + 10, 32:40, :] = strip
            for r, units, nexts in values:
                for u, value in enumerate(nexts):
                    target_vec[r + 10, 8 * u:8 * u + 8, :] = value
                if inside:
                    kept = nexts if step < 0 else units
                    for u in range(4):
                        at = 32 + 32 * step + 8 * u
                        basis[r, at:at + 8, :] = kept[u]

        def outer_rows(i, reach=reach):
            return (2 * i - reach, 2 * i - reach + 1, NR + 2 * i, NR + 2 * i + 1)

        def middle_rows(i):
            return tuple(4 * i + j for j in range(4))

        def outer(i, carry, some_rows=some_rows, outer_rows=outer_rows):
            some_rows(outer_rows(i), outer_rows(jnp.maximum(i - 1, 0)), False)
            return carry

        def middle(i, carry, some_rows=some_rows):
            some_rows(middle_rows(i), middle_rows(jnp.maximum(i - 1, 0)), True)
            return carry

        last = middle_rows(NR // 4 - 1)
        if reach > 0:
            lax.fori_loop(0, reach // 2, outer, 0)
            last = last + outer_rows(reach // 2 - 1)
        lax.fori_loop(0, NR // 4, middle, 0)
        if step + 1 < STEPS:
            mend(target_vec, last)

    sums[...] = jnp.zeros(sums.shape, F32)

    def product(i, carry):
        total = None
        for j in range(2):
            r = 4 * i + 2 * j
            high, mid, low = split(jnp.concatenate([basis[r], basis[r + 1]], axis=1))
            left = [jnp.concatenate([x[0:32], x[96:160]], axis=0) for x in (high, mid, low)]
            both = jnp.concatenate([high[32:], mid[32:]], axis=0)
            hh = matmul_t(left[0], both)
            mm = matmul_t(left[1], both)
            rest = matmul_t(left[2], high[32:]) + matmul_t(left[0], low[32:])
            part = ((rest + mm[:, NC:]) + (hh[:, NC:] + mm[:, :NC])) + hh[:, :NC]
            total = part if total is None else total + part
        sums[...] += total
        return carry

    lax.fori_loop(0, NR // 4, product, 0)
    lane = lanes((32, NC))
    low_half = sums[0:32, :] * scale
    high_half = jnp.where(lane < 64, turn(sums[32:64, :], -32), sums[64:96, :]) * scale
    row = lax.broadcasted_iota(jnp.int32, (32, NC), 0)
    within = lane % 32
    packed[0:32, :] = jnp.where(within >= row, low_half, high_half)
    diagonal = jnp.sum(jnp.where(within == row, high_half, 0.0), axis=0, keepdims=True)
    packed[32:40, :] = jnp.broadcast_to(diagonal, (8, NC))


def split(value):
    high = value.astype(jnp.bfloat16)
    value = value - high.astype(F32)
    mid = value.astype(jnp.bfloat16)
    return high, mid, (value - mid.astype(F32)).astype(jnp.bfloat16)


def matmul_t(a, b):
    return lax.dot_general(a, b, (((1,), (1,)), ((), ())), preferred_element_type=F32)


def matmul(a, b):
    return lax.dot_general(a, b, (((1,), (0,)), ((), ())), preferred_element_type=F32)


def exact_matmul(a, b):
    return lax.dot_general(a, b, (((1,), (0,)), ((), ())), precision=lax.Precision.HIGHEST,
                           preferred_element_type=F32)


def solve_body(parts, basis, out, upper, raw):
    total = parts[0]
    for i in range(1, parts.shape[0]):
        total = total + parts[i]
    half = total[0:32]
    lane = lanes((32, NC))
    row = lax.broadcasted_iota(jnp.int32, (32, NC), 0)
    within = lane % 32
    block = lane // 32
    flipped = jnp.transpose(jnp.concatenate([half] * 4, axis=0))
    mirror = flipped[0:32]
    for b in range(1, 4):
        mirror = jnp.where(block == b, flipped[32 * b:32 * b + 32], mirror)
    project = jnp.where(within >= row, half, mirror)
    later = jnp.where(within < row, half, jnp.where(within > row, mirror, jnp.broadcast_to(total[32:33], (32, NC))))
    early = project + 2.0 * turn(project, 32)
    gram = [
        jnp.where(block == 3, turn(later, -32), turn(early, -32)),
        jnp.where(block < 2, turn(early, 64), turn(later, 64)),
        jnp.where(block < 1, turn(early, 32), turn(later, 32)),
        later,
    ]
    right = [jnp.where(lane < 32, turn(project, -32 * b), 0.0) for b in range(4)]
    g = [gram[t // 4][8 * (t % 4):8 * (t % 4) + 8] for t in range(16)]
    p = [right[t // 4][8 * (t % 4):8 * (t % 4) + 8] for t in range(16)]
    lane = lanes((8, NC))
    sub = lax.broadcasted_iota(jnp.int32, (8, NC), 0)

    def spread(value, j):
        return jnp.broadcast_to(value[j:j + 1, :], (8, NC))

    def columns(value, base):
        return [jnp.broadcast_to(value[:, base + q:base + q + 1], (8, NC)) for q in range(8)]

    def panel(first):
        for t in range(first, first + 8):
            col = columns(g[t], 8 * t)
            steps = []
            for j in range(8):
                inverse = 1.0 / spread(col[j], j)
                raw[8 * t + j:8 * t + j + 1, :] = g[t][j:j + 1, :]
                u = spread(g[t], j) * inverse
                up = spread(p[t], j) * inverse
                m = jnp.where(sub == j, 0.0, col[j])
                scaled_cols = {}
                for q in range(j + 1, 8):
                    scaled_cols[q] = spread(col[q], j) * inverse
                    col[q] = col[q] - m * scaled_cols[q]
                g[t] = g[t] - m * u
                p[t] = p[t] - m * up
                steps.append((scaled_cols, u, up))
            for i in [first + (t - first + n) % 8 for n in range(1, 8)]:
                col = columns(g[i], 8 * t)
                for j in range(8):
                    scaled_cols, u, up = steps[j]
                    for q in range(j + 1, 8):
                        col[q] = col[q] - col[j] * scaled_cols[q]
                    g[i] = g[i] - col[j] * u
                    p[i] = p[i] - col[j] * up
        for t in range(first, first + 8):
            line = raw[8 * t:8 * t + 8, :]
            diagonal = jnp.sum(jnp.where(lane == sub + 8 * t, line, 0.0), axis=1, keepdims=True)
            diagonal = jnp.broadcast_to(diagonal, (8, NC))
            upper[8 * t:8 * t + 8, :] = jnp.where(lane >= sub + 8 * t, line / jnp.sqrt(diagonal), 0.0)
            inverse = 1.0 / diagonal
            g[t] = g[t] * inverse
            p[t] = p[t] * inverse

    below = jnp.concatenate(g[8:16], axis=0)[:, 0:64]
    panel(0)
    scaled = jnp.concatenate([jnp.concatenate(g[0:8], axis=0), jnp.concatenate(p[0:8], axis=0)], axis=1)
    update = exact_matmul(below, scaled)
    for t in range(8, 16):
        g[t] = g[t] - update[8 * t - 64:8 * t - 56, 0:NC]
        p[t] = p[t] - update[8 * t - 64:8 * t - 56, NC:]
    panel(8)
    last = jnp.concatenate(p[8:16], axis=0)
    above = turn(scaled[:, 0:NC], 64)[:, 0:64]
    first = scaled[:, NC:] - exact_matmul(above, last)
    weights = jnp.transpose(jnp.concatenate([first, last], axis=0))[0:32]
    high, mid, low = split(weights)
    left_a = jnp.concatenate([jnp.concatenate([high, high], axis=1), jnp.concatenate([mid, mid], axis=1)], axis=0)
    left_b = jnp.concatenate([high, low], axis=1)
    for r in range(0, NR, 2):
        w_high, w_mid, w_low = split(jnp.concatenate([basis[r, 32:160, :], basis[r + 1, 32:160, :]], axis=1))
        moved_a = matmul(left_a, jnp.concatenate([w_high, w_mid], axis=0))
        moved_b = matmul(left_b, jnp.concatenate([w_low, w_high], axis=0))
        moved = moved_a[0:32] + (moved_a[32:64] + moved_b)
        out[pl.ds(r, 32, stride=NR), :] = basis[r, 0:32, :] - moved[:, :NC]
        out[pl.ds(r + 1, 32, stride=NR), :] = basis[r + 1, 0:32, :] - moved[:, NC:]


def far(*dims):
    return jax.ShapeDtypeStruct(dims, F32)


def shape(*dims):
    return far(*dims) if INTERPRET else pltpu.VMEM(dims, F32)


def ring(count, step):
    return [(i, (i + step) % count) for i in range(count)]


def on_device(dom, sub, dom_count, sub_count, reduce_groups, source, initial, lumped_mass, node_slots, stiffness):
    rows_total, cols_total = dom_count * NR, sub_count * NC

    def prepare(*refs):
        prepare_body(dom, sub, rows_total, cols_total, *refs)

    ini_m, src_m, ini_h, src_h, w_main, w_strip, to_left, to_right, to_up, to_down = call(
        prepare,
        (shape(NR, NF, NC), shape(NR, NF, NC), shape(NR, 8, NC), shape(NR, 8, NC), shape(NH, 24, NC), shape(4, 24, NC),
         shape(176, NC), shape(176, NC), shape(MAIN_END, NC), shape(MAIN_END, NC)),
        scratch=[
            pltpu.VMEM((3, NH, 24, NC), F32),
            pltpu.VMEM((NF * NR, NC), F32),
            pltpu.VMEM((NF * NR, NC), F32),
            pltpu.VMEM((NR, NC), F32),
            pltpu.VMEM((6, NR, NC), jnp.int32),
            pltpu.VMEM((36, NR, NC), F32),
            pltpu.SemaphoreType.DMA((5,)),
        ],
        in_specs=[pl.BlockSpec(memory_space=pl.ANY)] * 5,
        name="prepare",
    )(*distant(source.reshape(NF * NR, NC), initial.reshape(NF * NR, NC), lumped_mass, node_slots,
               stiffness.reshape(36, NR, NC)))
    from_right = lax.ppermute(to_left, sub, ring(sub_count, -1))
    from_left = lax.ppermute(to_right, sub, ring(sub_count, 1))
    down_main = lax.ppermute(to_up, dom, ring(dom_count, -1))
    up_main = lax.ppermute(to_down, dom, ring(dom_count, 1))

    def columns(*refs):
        columns_body(sub, sub_count, *refs)

    ini_h, src_h, w_strip, to_up, to_down = call(
        columns,
        (shape(NR, 8, NC), shape(NR, 8, NC), shape(4, 24, NC), shape(STRIP_END, NC), shape(STRIP_END, NC)),
        name="columns",
    )(*near(ini_h, src_h, w_strip, from_left, from_right))
    down_strip = lax.ppermute(to_up, dom, ring(dom_count, -1))
    up_strip = lax.ppermute(to_down, dom, ring(dom_count, 1))

    def products(*refs):
        basis_body(dom, dom_count, 1.0 / float(rows_total * cols_total), *refs)

    basis, packed = call(
        products,
        (shape(NR, 160, NC), shape(40, NC)),
        scratch=[
            pltpu.VMEM((NCOEF, 40, NC), F32),
            pltpu.VMEM((NCOEF, 40, NC), F32),
            pltpu.VMEM((36, 40, NC), F32),
            pltpu.VMEM((36, 40, NC), F32),
            pltpu.VMEM((36, 40, NC), F32),
            pltpu.VMEM((96, NC), F32),
        ],
        name="products",
    )(*near(ini_m, src_m, ini_h, src_h, w_main, w_strip, up_main, down_main, up_strip, down_strip))
    for i, (axes, count) in enumerate(reduce_groups):
        if count == 2:
            gathered = jnp.stack([packed, lax.ppermute(packed, axes, [(0, 1), (1, 0)])])
        else:
            gathered = lax.all_to_all(jnp.broadcast_to(packed[None], (count, 40, NC)), axes, 0, 0)
        if i + 1 < len(reduce_groups):
            packed = jnp.sum(gathered, axis=0)
    new_residual, upper = call(
        solve_body,
        (far(NF * NR, NC), far(128, 128)),
        scratch=[pltpu.VMEM((128, NC), F32)],
        name="solve",
    )(*near(gathered, basis))
    return (new_residual.reshape(NF, NR, NC), upper)


def solution(mesh):
    dom_count, sub_count = mesh.shape["dom"], mesh.shape["sub"]
    if dom_count == 64 and sub_count == 4:
        fine = Mesh(mesh.devices.reshape(8, 4, 2, 4), ("z", "x", "c", "sub"))
        dom = ("z", "x", "c")
        groups = ((("c",), 2), (("x", "sub"), 16), (("z",), 8))
    else:
        fine, dom = mesh, ("dom",)
        groups = (("sub", sub_count), ("dom", dom_count))

    def body(*args):
        return on_device(dom, "sub", dom_count, sub_count, groups, *args)

    return jax.shard_map(
        body,
        mesh=fine,
        in_specs=(
            P(None, dom, "sub"),
            P(None, dom, "sub"),
            P(dom, "sub"),
            P(None, dom, "sub"),
            P(None, None, dom, "sub"),
        ),
        out_specs=(P(None, dom, "sub"), P()),
        check_vma=False,
    )
```

```python
import jax
import jax.numpy as jnp
from jax import lax
from jax.experimental import pallas as pl
from jax.experimental.pallas import tpu as pltpu
from jax.sharding import Mesh, PartitionSpec as P


STEPS = 4
NF = 32
NR = 16
NC = 128
INTERPRET = False
F32 = jnp.float32

HALF = [(0, 0), (0, 1), (0, 2)] + [(dr, dc) for dr in (1, 2) for dc in range(-2, 3)]
HALF_INDEX = {d: i for i, d in enumerate(HALF)}
NH = len(HALF)
TURNED = [d for d in HALF if d[1] != 0]
TURNED_INDEX = {d: NH + i for i, d in enumerate(TURNED)}
NCOEF = NH + len(TURNED)


def lanes(shape):
    return lax.broadcasted_iota(jnp.int32, shape, len(shape) - 1)


def turn(value, shift):
    shift = shift % NC
    return value if shift == 0 else pltpu.roll(value, shift, value.ndim - 1)


def call(body, outs, scratch=(), **kw):
    return pl.pallas_call(
        body,
        out_shape=outs,
        scratch_shapes=scratch,
        interpret=INTERPRET,
        compiler_params=pltpu.CompilerParams(vmem_limit_bytes=16 << 20),
        **kw,
    )


def near(*values):
    if INTERPRET:
        return values
    return tuple(pltpu.with_memory_space_constraint(v, pltpu.VMEM) for v in values)


def distant(*values):
    if INTERPRET:
        return values
    return tuple(pltpu.with_memory_space_constraint(v, pltpu.HBM) for v in values)


MAIN_I = 0
MAIN_S = 10 * 32
MAIN_W = MAIN_S + 8 * 32
MAIN_END = MAIN_W + NH * 16
STRIP_I = 0
STRIP_S = 10 * 8
STRIP_W = STRIP_S + 8 * 8
STRIP_END = STRIP_W + 4 * 16


def prepare_body(dom, sub_axis, rows_total, cols_total, source_far, initial_far, mass_far, slots_far, stiffness_far,
                 ini_m, src_m, ini_h, src_h, w_main, w_strip, to_left, to_right, to_up, to_down,
                 acc, source, initial, mass, slots, stiffness, arrived):
    copies = [
        pltpu.make_async_copy(far_ref, near_ref, arrived.at[i])
        for i, (far_ref, near_ref) in enumerate((
            (slots_far, slots), (stiffness_far, stiffness), (mass_far, mass), (initial_far, initial),
            (source_far, source)))
    ]
    for copy in copies:
        copy.start()
    for copy in copies[:3]:
        copy.wait()
    row = lax.broadcasted_iota(jnp.int32, (NR, NC), 0) + lax.axis_index(dom) * NR
    col = lanes((NR, NC)) + lax.axis_index(sub_axis) * NC
    top, bottom = row == 0, row == rows_total - 1
    west, east = col == 0, col == cols_total - 1
    kept = []
    for a in range(6):
        slot = slots[a]
        in_west = (slot == 0) | (slot == 3) | (slot == 6)
        in_east = (slot == 2) | (slot == 5) | (slot == 8)
        outside = (top & (slot < 3)) | (bottom & (slot > 5)) | (west & in_west) | (east & in_east)
        kept.append(jnp.where(outside, 99, slot))
    acc[...] = jnp.zeros(acc.shape, F32)
    zero = jnp.zeros((NR, NC), F32)
    for q in range(9):
        middle = []
        for a in range(6):
            value = zero
            for b in range(6):
                value = jnp.where(kept[b] == q, stiffness[a * 6 + b], value)
            middle.append(value)
        for p in range(q + 1):
            value = zero
            for a in range(6):
                value = jnp.where(kept[a] == p, middle[a], value)
            place = HALF_INDEX[(q // 3 - p // 3, q % 3 - p % 3)]
            start = 7 + p // 3 - 1
            acc[p % 3, place, start:start + NR, :] += value
    acc[1, 0, 7:7 + NR, :] += mass[...]

    lane = lanes((24, NC))
    pack_left = [jnp.zeros((24, NC), F32) for _ in range(2)]
    pack_right = [jnp.zeros((24, NC), F32) for _ in range(2)]
    strips = [jnp.zeros((24, NC), F32) for _ in range(4)]
    for d in range(NH):
        east_turn = turn(acc[2, d], 1)
        west_turn = turn(acc[0, d], -1)
        over_east = jnp.where(lane == 0, east_turn, 0.0)
        over_west = jnp.where(lane == NC - 1, west_turn, 0.0)
        main = acc[1, d] + (east_turn - over_east) + (west_turn - over_west)
        w_main[d] = main
        to_up[MAIN_W + 16 * d:MAIN_W + 16 * d + 16, :] = main[0:16]
        to_down[MAIN_W + 16 * d:MAIN_W + 16 * d + 16, :] = main[8:24]
        own = turn(jnp.where(lane < 4, main, 0.0) + over_west, 28)
        own = own + turn(jnp.where(lane >= 124, main, 0.0) + over_east, 4)
        strips[d // 4] = strips[d // 4] + turn(own, 32 * (d % 4))
        k = 16 * (d % 8)
        pack_right[d // 8] = pack_right[d // 8] + turn(jnp.where(lane >= 118, main, 0.0) + over_east, 12 + k)
        pack_left[d // 8] = pack_left[d // 8] + turn(jnp.where(lane < 10, main, 0.0) + over_west, 4 + k)
    for j in range(4):
        w_strip[j] = strips[j]
    for j in range(2):
        to_right[128 + 24 * j:152 + 24 * j, :] = pack_right[j]
        to_left[128 + 24 * j:152 + 24 * j, :] = pack_left[j]

    for copy in copies[3:]:
        copy.wait()
    lane = lanes((8, NC))
    place = lane % 32
    second = (lane >= 16) & (lane < 48)
    upper_pair = (lane >= 48) & (lane < 112)

    def edges(tiles):
        low = jnp.where(second, turn(tiles[1], 32), tiles[0])
        high = jnp.where(second, turn(tiles[3], 32), tiles[2])
        return jnp.where(upper_pair, turn(high, 64), low)

    zero = jnp.zeros((8, NC), F32)
    for r in range(NR):
        inis = [initial[pl.ds(g * 128 + r, 8, stride=NR), :] for g in range(4)]
        srcs = [source[pl.ds(g * 128 + r, 8, stride=NR), :] for g in range(4)]
        for g in range(4):
            at, ini, src = 8 * g, inis[g], srcs[g]
            ini_m[r, at:at + 8, :] = ini
            src_m[r, at:at + 8, :] = src
            if r < 10:
                to_up[MAIN_I + 32 * r + at:MAIN_I + 32 * r + at + 8, :] = ini
            if r >= 6:
                to_down[MAIN_I + 32 * (r - 6) + at:MAIN_I + 32 * (r - 6) + at + 8, :] = ini
            if r < 8:
                to_up[MAIN_S + 32 * r + at:MAIN_S + 32 * r + at + 8, :] = src
            else:
                to_down[MAIN_S + 32 * (r - 8) + at:MAIN_S + 32 * (r - 8) + at + 8, :] = src
        ini, src = edges(inis), edges(srcs)
        ini_east, ini_west, src_east, src_west = turn(ini, 4), turn(ini, 28), turn(src, 4), turn(src, 28)
        strip_i = jnp.where(place < 4, ini_east, jnp.where(place >= 28, ini_west, zero))
        strip_s = jnp.where(place < 4, src_east, jnp.where(place >= 28, src_west, zero))
        left = jnp.where((place >= 4) & (place < 14), ini_east, turn(src, 20))
        left = jnp.where((place >= 4) & (place < 30), left, zero)
        right = jnp.where((place >= 18) & (place < 28), src_west, turn(ini, 12))
        right = jnp.where((place >= 2) & (place < 28), right, zero)
        ini_h[r] = strip_i
        src_h[r] = strip_s
        to_right[8 * r:8 * r + 8, :] = right
        to_left[8 * r:8 * r + 8, :] = left


def columns_body(sub_axis, sub_count, ini_h, src_h, w_strip, from_left, from_right, ini_o, src_o, strip_o, to_up, to_down):
    lane = lanes((8, NC))
    place = lane % 32
    is_left = (place >= 18) & (place < 28)
    is_right = (place >= 4) & (place < 14)
    at = lax.axis_index(sub_axis)
    has_left, has_right = at > 0, at < sub_count - 1
    for r in range(NR):
        left = jnp.where(has_left, from_left[8 * r:8 * r + 8, :], 0.0)
        right = jnp.where(has_right, from_right[8 * r:8 * r + 8, :], 0.0)
        ini = jnp.where(is_left, turn(left, 16), jnp.where(is_right, right, ini_h[r]))
        src = jnp.where(is_left, left, jnp.where(is_right, turn(right, -16), src_h[r]))
        ini_o[r] = ini
        src_o[r] = src
        if r < 10:
            to_up[STRIP_I + 8 * r:STRIP_I + 8 * r + 8, :] = ini
        if r >= 6:
            to_down[STRIP_I + 8 * (r - 6):STRIP_I + 8 * (r - 6) + 8, :] = ini
        if r < 8:
            to_up[STRIP_S + 8 * r:STRIP_S + 8 * r + 8, :] = src
        else:
            to_down[STRIP_S + 8 * (r - 8):STRIP_S + 8 * (r - 8) + 8, :] = src
    lane = lanes((24, NC))
    strips = [w_strip[j] for j in range(4)]
    for d in range(NH):
        k = 16 * (d % 8)
        left = from_left[128 + 24 * (d // 8):152 + 24 * (d // 8), :]
        right = from_right[128 + 24 * (d // 8):152 + 24 * (d // 8), :]
        left = jnp.where((lane >= 18) & (lane <= 28) & has_left, turn(left, 16 - k), 0.0)
        right = jnp.where((lane >= 3) & (lane <= 13) & has_right, turn(right, -k), 0.0)
        strips[d // 4] = strips[d // 4] + turn(left + right, 32 * (d % 4))
    for j in range(4):
        strip_o[j] = strips[j]
        to_up[STRIP_W + 16 * j:STRIP_W + 16 * j + 16, :] = strips[j][0:16]
        to_down[STRIP_W + 16 * j:STRIP_W + 16 * j + 16, :] = strips[j][8:24]


def basis_body(dom, dom_count, scale, ini_m, src_m, ini_h, src_h, w_main, w_strip, up_main, down_main, up_strip, down_strip,
               basis, packed,
               coef_m, coef_h, ini_v, src_v, vec_a, vec_b, sums):
    lane = lanes((8, NC))
    segment = lane // 32
    own = (1, 2, 3)
    at = lax.axis_index(dom)
    has_up, has_down = at > 0, at < dom_count - 1

    def upper(ref, start, size=8):
        return jnp.where(has_up, ref[start:start + size, :], 0.0)

    def lower(ref, start, size=8):
        return jnp.where(has_down, ref[start:start + size, :], 0.0)

    for t in range(5):
        for d in range(NH):
            main = None
            strip = None
            parts = []
            if t < 2:
                parts.append((upper(up_main, MAIN_W + 16 * d + 8 * t), upper(up_strip, STRIP_W + 16 * (d // 4) + 8 * t)))
            if t in own:
                parts.append((w_main[d, 8 * t - 8:8 * t, :], w_strip[d // 4, 8 * t - 8:8 * t, :]))
            if t > 2:
                s = 8 * (t - 3)
                parts.append((lower(down_main, MAIN_W + 16 * d + s), lower(down_strip, STRIP_W + 16 * (d // 4) + s)))
            main = sum(p[0] for p in parts[1:]) + parts[0][0] if len(parts) > 1 else parts[0][0]
            strip = sum(p[1] for p in parts[1:]) + parts[0][1] if len(parts) > 1 else parts[0][1]
            if d % 4 == 0:
                packed_strip = [turn(strip, 32 * n) for n in range(4)]
            strip = packed_strip[(3 - d) % 4]
            for n in range(3):
                strip = jnp.where(segment == n, packed_strip[(n - d) % 4], strip)
            west, east = turn(strip, -28), turn(strip, -4)
            main = jnp.where(lane == 0, west, jnp.where(lane == NC - 1, east, main))
            coef_m[d, 8 * t:8 * t + 8, :] = main
            coef_h[d, 8 * t:8 * t + 8, :] = strip
            dc = HALF[d][1]
            if dc != 0:
                beyond = jnp.where(lane >= 126, west, main) if dc > 0 else jnp.where(lane < 2, east, main)
                i = TURNED_INDEX[HALF[d]]
                coef_m[i, 8 * t:8 * t + 8, :] = turn(beyond, dc)
                coef_h[i, 8 * t:8 * t + 8, :] = turn(strip, dc)

    for i in range(10):
        ini_v[i, 0:32] = upper(up_main, MAIN_I + 32 * i, 32)
        ini_v[i, 32:40] = upper(up_strip, STRIP_I + 8 * i)
        ini_v[26 + i, 0:32] = lower(down_main, MAIN_I + 32 * i, 32)
        ini_v[26 + i, 32:40] = lower(down_strip, STRIP_I + 8 * i)
    for i in range(8):
        src_v[2 + i, 0:32] = upper(up_main, MAIN_S + 32 * i, 32)
        src_v[2 + i, 32:40] = upper(up_strip, STRIP_S + 8 * i)
        src_v[26 + i, 0:32] = lower(down_main, MAIN_S + 32 * i, 32)
        src_v[26 + i, 32:40] = lower(down_strip, STRIP_S + 8 * i)
    for i in range(NR):
        ini_v[10 + i, 0:32] = ini_m[i]
        ini_v[10 + i, 32:40] = ini_h[i]
        src_v[10 + i, 0:32] = src_m[i]
        src_v[10 + i, 32:40] = src_h[i]

    place = lane % 32
    edge = (lane < 2) | (lane >= NC - 2)
    from_low = place < 2
    tail = place >= 30
    second = (lane >= 16) & (lane < 48)
    upper_pair = (lane >= 48) & (lane < 112)

    def edges_of(strip):
        both = jnp.where(from_low, turn(strip, -28), turn(strip, -4))
        return [turn(both, -32 * g) for g in range(4)]

    def inner_of(mains, strip):
        low = jnp.where(second, turn(mains[1], 32), mains[0])
        high = jnp.where(second, turn(mains[3], 32), mains[2])
        both = jnp.where(upper_pair, turn(high, 64), low)
        return jnp.where(tail, turn(both, 28), jnp.where(from_low, turn(both, 4), strip))

    def image(vec, r):
        def spread(ref):
            coef = {}
            for dr in range(-2, 3):
                for dc in range(-2, 3):
                    if (dr, dc) in HALF_INDEX:
                        index = TURNED_INDEX[(dr, dc)] if dc != 0 else HALF_INDEX[(dr, dc)]
                        at = r + 15
                    else:
                        index = HALF_INDEX[(-dr, -dc)]
                        at = r + 15 + dr
                    coef[(dr, dc)] = jnp.broadcast_to(ref[index, pl.ds(at, 1), :], (8, NC))
            return coef

        def unit(coef, u):
            near = [vec[r + 10 + dr, 8 * u:8 * u + 8, :] for dr in range(-2, 3)]
            parts = []
            for dc in (-2, 2, -1, 1, 0):
                part = None
                for dr in range(-2, 3):
                    term = coef[(dr, dc)] * near[dr + 2]
                    part = term if part is None else part + term
                parts.append(turn(part, -dc))
            return ((parts[0] + parts[1]) + (parts[2] + parts[3])) + parts[4]

        strip = unit(spread(coef_h), 4)
        coef = spread(coef_m)
        edges = edges_of(strip)
        result = [jnp.where(edge, edges[g], unit(coef, g)) for g in range(4)]
        return result + [strip]

    def mended(vec, r):
        mains = [vec[r + 10, 8 * g:8 * g + 8, :] for g in range(4)]
        return inner_of(mains, vec[r + 10, 32:40, :])

    def mend(vec, rows):
        strips = [mended(vec, r) for r in rows]
        for r, strip in zip(rows, strips):
            vec[r + 10, 32:40, :] = strip

    vectors = (vec_a, vec_b)
    for step in range(-1, STEPS):
        reach = 6 - 2 * step
        source_vec = ini_v if step < 0 else vectors[step % 2]
        target_vec = vec_a if step < 0 else vectors[(step + 1) % 2]

        def some_rows(rows, before, inside, step=step, source_vec=source_vec, target_vec=target_vec):
            more = step + 1 < STEPS
            strips = [mended(target_vec, r) for r in before] if more else []
            values = []
            for r in rows:
                units = image(source_vec, r)
                olds = src_v if step < 0 else source_vec
                nexts = []
                if more:
                    for u in range(5):
                        old = olds[r + 10, 8 * u:8 * u + 8, :]
                        nexts.append(old - units[u] if step < 0 else units[u] - 2.0 * old)
                values.append((r, units, nexts))
            for r, strip in zip(before, strips):
                target_vec[r + 10, 32:40, :] = strip
            for r, units, nexts in values:
                for u, value in enumerate(nexts):
                    target_vec[r + 10, 8 * u:8 * u + 8, :] = value
                if inside:
                    kept = nexts if step < 0 else units
                    for u in range(4):
                        at = 32 + 32 * step + 8 * u
                        basis[r, at:at + 8, :] = kept[u]

        def outer_rows(i, reach=reach):
            return (2 * i - reach, 2 * i - reach + 1, NR + 2 * i, NR + 2 * i + 1)

        def middle_rows(i):
            return tuple(4 * i + j for j in range(4))

        def outer(i, carry, some_rows=some_rows, outer_rows=outer_rows):
            some_rows(outer_rows(i), outer_rows(jnp.maximum(i - 1, 0)), False)
            return carry

        def middle(i, carry, some_rows=some_rows):
            some_rows(middle_rows(i), middle_rows(jnp.maximum(i - 1, 0)), True)
            return carry

        last = middle_rows(NR // 4 - 1)
        if reach > 0:
            lax.fori_loop(0, reach // 2, outer, 0)
            last = last + outer_rows(reach // 2 - 1)
        lax.fori_loop(0, NR // 4, middle, 0)
        if step + 1 < STEPS:
            mend(target_vec, last)

    sums[...] = jnp.zeros(sums.shape, F32)

    def product(i, carry):
        total = None
        for j in range(2):
            r = 4 * i + 2 * j
            high, mid, low = split(jnp.concatenate([basis[r], basis[r + 1]], axis=1))
            left = [jnp.concatenate([x[0:32], x[96:160]], axis=0) for x in (high, mid, low)]
            both = jnp.concatenate([high[32:], mid[32:]], axis=0)
            hh = matmul_t(left[0], both)
            mm = matmul_t(left[1], both)
            rest = matmul_t(left[2], high[32:]) + matmul_t(left[0], low[32:])
            part = ((rest + mm[:, NC:]) + (hh[:, NC:] + mm[:, :NC])) + hh[:, :NC]
            total = part if total is None else total + part
        sums[...] += total
        return carry

    lax.fori_loop(0, NR // 4, product, 0)
    lane = lanes((32, NC))
    low_half = sums[0:32, :] * scale
    high_half = jnp.where(lane < 64, turn(sums[32:64, :], -32), sums[64:96, :]) * scale
    row = lax.broadcasted_iota(jnp.int32, (32, NC), 0)
    within = lane % 32
    packed[0:32, :] = jnp.where(within >= row, low_half, high_half)
    diagonal = jnp.sum(jnp.where(within == row, high_half, 0.0), axis=0, keepdims=True)
    packed[32:40, :] = jnp.broadcast_to(diagonal, (8, NC))


def split(value):
    high = value.astype(jnp.bfloat16)
    value = value - high.astype(F32)
    mid = value.astype(jnp.bfloat16)
    return high, mid, (value - mid.astype(F32)).astype(jnp.bfloat16)


def matmul_t(a, b):
    return lax.dot_general(a, b, (((1,), (1,)), ((), ())), preferred_element_type=F32)


def matmul(a, b):
    return lax.dot_general(a, b, (((1,), (0,)), ((), ())), preferred_element_type=F32)


def exact_matmul(a, b):
    return lax.dot_general(a, b, (((1,), (0,)), ((), ())), precision=lax.Precision.HIGHEST,
                           preferred_element_type=F32)


def solve_body(parts, basis, out, upper, raw):
    total = parts[0]
    for i in range(1, parts.shape[0]):
        total = total + parts[i]
    half = total[0:32]
    lane = lanes((32, NC))
    row = lax.broadcasted_iota(jnp.int32, (32, NC), 0)
    within = lane % 32
    block = lane // 32
    flipped = jnp.transpose(jnp.concatenate([half] * 4, axis=0))
    mirror = flipped[0:32]
    for b in range(1, 4):
        mirror = jnp.where(block == b, flipped[32 * b:32 * b + 32], mirror)
    project = jnp.where(within >= row, half, mirror)
    later = jnp.where(within < row, half, jnp.where(within > row, mirror, jnp.broadcast_to(total[32:33], (32, NC))))
    early = project + 2.0 * turn(project, 32)
    gram = [
        jnp.where(block == 3, turn(later, -32), turn(early, -32)),
        jnp.where(block < 2, turn(early, 64), turn(later, 64)),
        jnp.where(block < 1, turn(early, 32), turn(later, 32)),
        later,
    ]
    right = [jnp.where(lane < 32, turn(project, -32 * b), 0.0) for b in range(4)]
    g = [gram[t // 4][8 * (t % 4):8 * (t % 4) + 8] for t in range(16)]
    p = [right[t // 4][8 * (t % 4):8 * (t % 4) + 8] for t in range(16)]
    lane = lanes((8, NC))
    sub = lax.broadcasted_iota(jnp.int32, (8, NC), 0)

    def spread(value, j):
        return jnp.broadcast_to(value[j:j + 1, :], (8, NC))

    def columns(value, base):
        return [jnp.broadcast_to(value[:, base + q:base + q + 1], (8, NC)) for q in range(8)]

    def panel(first):
        for t in range(first, first + 8):
            col = columns(g[t], 8 * t)
            steps = []
            for j in range(8):
                inverse = 1.0 / spread(col[j], j)
                raw[8 * t + j:8 * t + j + 1, :] = g[t][j:j + 1, :]
                u = spread(g[t], j) * inverse
                up = spread(p[t], j) * inverse
                m = jnp.where(sub == j, 0.0, col[j])
                scaled_cols = {}
                for q in range(j + 1, 8):
                    scaled_cols[q] = spread(col[q], j) * inverse
                    col[q] = col[q] - m * scaled_cols[q]
                g[t] = g[t] - m * u
                p[t] = p[t] - m * up
                steps.append((scaled_cols, u, up))
            for i in [first + (t - first + n) % 8 for n in range(1, 8)]:
                col = columns(g[i], 8 * t)
                for j in range(8):
                    scaled_cols, u, up = steps[j]
                    for q in range(j + 1, 8):
                        col[q] = col[q] - col[j] * scaled_cols[q]
                    g[i] = g[i] - col[j] * u
                    p[i] = p[i] - col[j] * up
        for t in range(first, first + 8):
            line = raw[8 * t:8 * t + 8, :]
            diagonal = jnp.sum(jnp.where(lane == sub + 8 * t, line, 0.0), axis=1, keepdims=True)
            diagonal = jnp.broadcast_to(diagonal, (8, NC))
            upper[8 * t:8 * t + 8, :] = jnp.where(lane >= sub + 8 * t, line / jnp.sqrt(diagonal), 0.0)
            inverse = 1.0 / diagonal
            g[t] = g[t] * inverse
            p[t] = p[t] * inverse

    below = jnp.concatenate(g[8:16], axis=0)[:, 0:64]
    panel(0)
    scaled = jnp.concatenate([jnp.concatenate(g[0:8], axis=0), jnp.concatenate(p[0:8], axis=0)], axis=1)
    update = exact_matmul(below, scaled)
    for t in range(8, 16):
        g[t] = g[t] - update[8 * t - 64:8 * t - 56, 0:NC]
        p[t] = p[t] - update[8 * t - 64:8 * t - 56, NC:]
    panel(8)
    last = jnp.concatenate(p[8:16], axis=0)
    above = turn(scaled[:, 0:NC], 64)[:, 0:64]
    first = scaled[:, NC:] - exact_matmul(above, last)
    weights = jnp.transpose(jnp.concatenate([first, last], axis=0))[0:32]
    high, mid, low = split(weights)
    left_a = jnp.concatenate([jnp.concatenate([high, high], axis=1), jnp.concatenate([mid, mid], axis=1)], axis=0)
    left_b = jnp.concatenate([high, low], axis=1)
    for r in range(0, NR, 2):
        w_high, w_mid, w_low = split(jnp.concatenate([basis[r, 32:160, :], basis[r + 1, 32:160, :]], axis=1))
        moved_a = matmul(left_a, jnp.concatenate([w_high, w_mid], axis=0))
        moved_b = matmul(left_b, jnp.concatenate([w_low, w_high], axis=0))
        moved = moved_a[0:32] + (moved_a[32:64] + moved_b)
        out[pl.ds(r, 32, stride=NR), :] = basis[r, 0:32, :] - moved[:, :NC]
        out[pl.ds(r + 1, 32, stride=NR), :] = basis[r + 1, 0:32, :] - moved[:, NC:]


def far(*dims):
    return jax.ShapeDtypeStruct(dims, F32)


def shape(*dims):
    return far(*dims) if INTERPRET else pltpu.VMEM(dims, F32)


def ring(count, step):
    return [(i, (i + step) % count) for i in range(count)]


def on_device(dom, sub, dom_count, sub_count, reduce_groups, source, initial, lumped_mass, node_slots, stiffness):
    rows_total, cols_total = dom_count * NR, sub_count * NC

    def prepare(*refs):
        prepare_body(dom, sub, rows_total, cols_total, *refs)

    ini_m, src_m, ini_h, src_h, w_main, w_strip, to_left, to_right, to_up, to_down = call(
        prepare,
        (shape(NR, NF, NC), shape(NR, NF, NC), shape(NR, 8, NC), shape(NR, 8, NC), shape(NH, 24, NC), shape(4, 24, NC),
         shape(176, NC), shape(176, NC), shape(MAIN_END, NC), shape(MAIN_END, NC)),
        scratch=[
            pltpu.VMEM((3, NH, 24, NC), F32),
            pltpu.VMEM((NF * NR, NC), F32),
            pltpu.VMEM((NF * NR, NC), F32),
            pltpu.VMEM((NR, NC), F32),
            pltpu.VMEM((6, NR, NC), jnp.int32),
            pltpu.VMEM((36, NR, NC), F32),
            pltpu.SemaphoreType.DMA((5,)),
        ],
        in_specs=[pl.BlockSpec(memory_space=pl.ANY)] * 5,
        name="prepare",
    )(*distant(source.reshape(NF * NR, NC), initial.reshape(NF * NR, NC), lumped_mass, node_slots,
               stiffness.reshape(36, NR, NC)))
    from_right = lax.ppermute(to_left, sub, ring(sub_count, -1))
    from_left = lax.ppermute(to_right, sub, ring(sub_count, 1))
    down_main = lax.ppermute(to_up, dom, ring(dom_count, -1))
    up_main = lax.ppermute(to_down, dom, ring(dom_count, 1))

    def columns(*refs):
        columns_body(sub, sub_count, *refs)

    ini_h, src_h, w_strip, to_up, to_down = call(
        columns,
        (shape(NR, 8, NC), shape(NR, 8, NC), shape(4, 24, NC), shape(STRIP_END, NC), shape(STRIP_END, NC)),
        name="columns",
    )(*near(ini_h, src_h, w_strip, from_left, from_right))
    down_strip = lax.ppermute(to_up, dom, ring(dom_count, -1))
    up_strip = lax.ppermute(to_down, dom, ring(dom_count, 1))

    def products(*refs):
        basis_body(dom, dom_count, 1.0 / float(rows_total * cols_total), *refs)

    basis, packed = call(
        products,
        (shape(NR, 160, NC), shape(40, NC)),
        scratch=[
            pltpu.VMEM((NCOEF, 40, NC), F32),
            pltpu.VMEM((NCOEF, 40, NC), F32),
            pltpu.VMEM((36, 40, NC), F32),
            pltpu.VMEM((36, 40, NC), F32),
            pltpu.VMEM((36, 40, NC), F32),
            pltpu.VMEM((36, 40, NC), F32),
            pltpu.VMEM((96, NC), F32),
        ],
        name="products",
    )(*near(ini_m, src_m, ini_h, src_h, w_main, w_strip, up_main, down_main, up_strip, down_strip))
    for i, (axes, count) in enumerate(reduce_groups):
        if count == 2:
            gathered = jnp.stack([packed, lax.ppermute(packed, axes, [(0, 1), (1, 0)])])
        else:
            gathered = lax.all_to_all(jnp.broadcast_to(packed[None], (count, 40, NC)), axes, 0, 0)
        if i + 1 < len(reduce_groups):
            packed = jnp.sum(gathered, axis=0)
    new_residual, upper = call(
        solve_body,
        (far(NF * NR, NC), far(128, 128)),
        scratch=[pltpu.VMEM((128, NC), F32)],
        name="solve",
    )(*near(gathered, basis))
    return (new_residual.reshape(NF, NR, NC), upper)


def solution(mesh):
    dom_count, sub_count = mesh.shape["dom"], mesh.shape["sub"]
    if dom_count == 64 and sub_count == 4:
        fine = Mesh(mesh.devices.reshape(8, 4, 2, 4), ("z", "x", "c", "sub"))
        dom = ("z", "x", "c")
        groups = ((("c",), 2), (("z",), 8), (("x", "sub"), 16))
    else:
        fine, dom = mesh, ("dom",)
        groups = (("sub", sub_count), ("dom", dom_count))

    def body(*args):
        return on_device(dom, "sub", dom_count, sub_count, groups, *args)

    return jax.shard_map(
        body,
        mesh=fine,
        in_specs=(
            P(None, dom, "sub"),
            P(None, dom, "sub"),
            P(dom, "sub"),
            P(None, dom, "sub"),
            P(None, None, dom, "sub"),
        ),
        out_specs=(P(None, dom, "sub"), P()),
        check_vma=False,
    )
```
